768 devices in a mesh: dp: 24 (over z_lo, x, core), mp: 32 (over z_hi, y).
Axes of the slice: x: 4, y: 8, z: 12 (z_hi: 4, z_lo: 3; z = z_hi * 3 + z_lo), core: 2. Of those that a mesh axis runs over, the one named last changes fastest.
Arguments:
- prelude_output: bfloat16 [72, 32, 5280], P('dp', None, 'mp'), may hold values from -6 to 6
- init_noise: bfloat16 [96, 32, 5280], P('dp', None, 'mp'), may hold values from -6 to 6
- core_weight: bfloat16 [5280, 5280], P('mp'), may hold values from -0.078125 to 0.078125
- norm_gain: float32 [5280], replicated, may hold values from 0.5 to 1.5
- state_cotangent: bfloat16 [96, 32, 5280], P('dp', None, 'mp'), may hold values from -6 to 6
- step_counts: int32 [72], replicated, may hold values from 1 to 3, as said below
- group_table: int32 [72], replicated, may hold values from 0 to 23, as said below
Outputs:
- weight_grad: float32 [5280, 5280], P('mp', 'dp')
The draws below stay inside these ranges and needn't reach their ends.
Inputs may be any that keep to these rules, and one draw needn't show every extreme that they name: `step_counts`: sequences in the groups that run fewer sequences all take 3 steps. `group_table`: half of the groups run 4 sequences and the other half run 2 (their other 2 slots stay empty).
All inputs are finite; a program needn't handle non-finite values.
Results may differ from the reference program's by a relative error of at most 0.025.
Values may be sent and summed in bfloat16 or wider, within the bound.
No kernel may reach another device: no remote copies, remote signals or barrier semaphores. Data moves between devices by JAX's collectives and lax.ppermute only.
A program may use at most 32 MiB of HBM per device.

```python
import jax
import jax.numpy as jnp
from jax import lax

MODEL_WIDTH = 5280
TOKEN_LENGTH = 32
SEQ_DEV = 3
CAP = 4
MAXR = 3
BP = 2
SEQS = 72
SEQUENCE_SLOTS = 96
N_DP = 24
N_MP = 32


def deal_sequences(key):
    base_key = jax.random.fold_in(key, 11)
    order_key, group_key, count_key = jax.random.split(base_key, 3)
    group_total = SEQS // SEQ_DEV
    group_halves = group_total // 2
    light_size = CAP
    heavy_size = 2 * SEQ_DEV - CAP
    heavy_total = group_halves * heavy_size
    seq_order = jax.random.permutation(order_key, SEQS).astype(jnp.int32)
    group_order = jax.random.permutation(group_key, group_total).astype(jnp.int32)
    position = jnp.arange(SEQS, dtype=jnp.int32)
    is_heavy = position < heavy_total
    heavy_slot = jnp.clip(position // heavy_size, 0, group_total - 1)
    light_slot = jnp.clip(group_halves + (position - heavy_total) // light_size, 0, group_total - 1)
    group_at = jnp.where(is_heavy, group_order[heavy_slot], group_order[light_slot])
    light_counts = jax.random.randint(count_key, (SEQS,), 1, MAXR).astype(jnp.int32)
    count_at = jnp.where(is_heavy, MAXR, light_counts).astype(jnp.int32)
    table = jnp.zeros((SEQS,), jnp.int32).at[seq_order].set(group_at)
    counts = jnp.zeros((SEQS,), jnp.int32).at[seq_order].set(count_at)
    return (counts, table)


def draw_step_counts(key, part):
    counts, table = deal_sequences(key)
    return counts


def draw_group_table(key, part):
    counts, table = deal_sequences(key)
    return table


def steps_of(rng, shape, shards, least, high):
    def one(dim, blocks):
        steps = jax.random.uniform(jax.random.fold_in(jax.random.fold_in(rng, 6), dim), (blocks,), jnp.float32, least / len(shards), high / len(shards))
        return jnp.repeat(jnp.exp(steps), shape[dim] // blocks).reshape((-1,) + (1,) * (len(shape) - dim - 1))

    gain = one(*shards[0])
    for cut in shards[1:]:
        gain = gain * one(*cut)
    return gain


def centred(own_key, dims, scale, bound, cuts=(), held_as=jnp.bfloat16):
    loudness = steps_of(own_key, dims, cuts, -0.22, 0.18) if cuts else 1.0
    array = jax.random.normal(own_key, dims, jnp.float32) * scale * loudness
    return jnp.minimum(jnp.maximum(array, -bound), bound).astype(held_as)


def setup_inputs(seed: int = 0) -> dict:
    keys = jax.random.split(jax.random.key(seed), 8)
    return {
        "prelude_output": centred(keys[0], (SEQS, TOKEN_LENGTH, MODEL_WIDTH), 1.0, 6.0, ((0, 24), (2, 32))),
        "init_noise": centred(keys[1], (SEQUENCE_SLOTS, TOKEN_LENGTH, MODEL_WIDTH), 1.0, 6.0, ((0, 24), (2, 32))),
        "core_weight": centred(keys[2], (MODEL_WIDTH, MODEL_WIDTH), MODEL_WIDTH ** -0.5, 0.078125, ((0, 32),)),
        "norm_gain": jnp.clip(1.0 + 0.1 * jax.random.normal(keys[3], (MODEL_WIDTH,), jnp.float32), 0.5, 1.5),
        "state_cotangent": centred(keys[4], (SEQUENCE_SLOTS, TOKEN_LENGTH, MODEL_WIDTH), 1.0, 6.0, ((0, 24), (2, 32))),
        "step_counts": draw_step_counts(jax.random.fold_in(keys[7], 71), 0),
        "group_table": draw_group_table(jax.random.fold_in(keys[7], 71), 0),
    }


EPS = 1e-06

def block_sum(delta_b, core_weight):
    block_width = MODEL_WIDTH // N_MP

    def add_block(running, block_index):
        first_row = block_index * block_width
        delta_cols = lax.dynamic_slice_in_dim(delta_b, first_row, block_width, 1)
        weight_rows = lax.dynamic_slice_in_dim(core_weight, first_row, block_width, 0)
        product = jnp.dot(delta_cols, weight_rows, preferred_element_type=jnp.float32)
        rounded = lax.optimization_barrier(product.astype(jnp.bfloat16)).astype(jnp.float32)
        return (running + rounded, None)
    start_value = jnp.zeros((delta_b.shape[0], MODEL_WIDTH), jnp.float32)
    finished, unused = lax.scan(add_block, start_value, jnp.arange(N_MP, dtype=jnp.int32))
    return finished

def reference(prelude_output, init_noise, core_weight, norm_gain, state_cotangent, step_counts, group_table):
    seq_index = jnp.arange(SEQS, dtype=jnp.int32)
    earlier = (group_table[:, None] == group_table[None, :]) & (seq_index[None, :] < seq_index[:, None])
    slot_rank = lax.optimization_barrier(jnp.sum(earlier.astype(jnp.int32), axis=1))
    placed = group_table * CAP + slot_rank
    slot_index = jnp.arange(SEQUENCE_SLOTS, dtype=jnp.int32)
    selected_rows = placed[None, :] == slot_index[:, None]
    injected_input = jnp.einsum('gu,uhv->ghv', selected_rows.astype(jnp.float32), prelude_output.astype(jnp.float32), precision=lax.Precision.HIGHEST).reshape(SEQUENCE_SLOTS * TOKEN_LENGTH, MODEL_WIDTH)
    slot_counts = lax.optimization_barrier(jnp.sum(jnp.where(selected_rows, step_counts[None, :], 0), axis=1))
    state = init_noise.reshape(SEQUENCE_SLOTS * TOKEN_LENGTH, MODEL_WIDTH)
    saved = []
    for turn in range(MAXR):
        active = jnp.repeat(turn >= MAXR - slot_counts, TOKEN_LENGTH)[:, None]
        product = lax.dot_general(state, core_weight, (((1,), (1,)), ((), ())), preferred_element_type=jnp.float32)
        mixed = (product + injected_input).astype(jnp.bfloat16)
        mixed_float = mixed.astype(jnp.float32)
        inverse_rms = lax.rsqrt(lax.optimization_barrier(jnp.sum(mixed_float * mixed_float, axis=1)) / MODEL_WIDTH + EPS)
        renewed = (norm_gain * mixed_float * inverse_rms[:, None]).astype(jnp.bfloat16)
        saved.append((state, mixed_float, inverse_rms, active))
        state = jnp.where(active, renewed, state)
    upstream = state_cotangent.reshape(SEQUENCE_SLOTS * TOKEN_LENGTH, MODEL_WIDTH).astype(jnp.float32)
    delta_list = []
    state_list = []
    for back_index in range(BP):
        state_in, mixed_float, inverse_rms, active = saved[MAXR - 1 - back_index]
        scaled = upstream * norm_gain
        inner = lax.optimization_barrier(jnp.sum(scaled * mixed_float, axis=1))
        delta = inverse_rms[:, None] * scaled - mixed_float * (inverse_rms ** 3 * inner / MODEL_WIDTH)[:, None]
        delta_b = jnp.where(active, delta, 0.0).astype(jnp.bfloat16)
        delta_list.append(delta_b)
        state_list.append(state_in)
        if back_index + 1 < BP:
            upstream = jnp.where(active, block_sum(delta_b, core_weight), upstream)
    group_rows = CAP * TOKEN_LENGTH
    deltas = jnp.stack(delta_list).reshape(BP, N_DP, group_rows, MODEL_WIDTH).transpose(1, 0, 2, 3)
    states = jnp.stack(state_list).reshape(BP, N_DP, group_rows, MODEL_WIDTH).transpose(1, 0, 2, 3)

    def add_group(total, pieces):
        group_deltas, group_states = pieces
        partial_grad = jnp.zeros((MODEL_WIDTH, MODEL_WIDTH), jnp.float32)
        for back_index in range(BP):
            partial_grad = partial_grad + lax.dot_general(group_deltas[back_index], group_states[back_index], (((0,), (0,)), ((), ())), preferred_element_type=jnp.float32)
        rounded = lax.optimization_barrier(partial_grad.astype(jnp.bfloat16)).astype(jnp.float32)
        return (total + rounded, None)
    weight_grad, unused = lax.scan(add_group, jnp.zeros((MODEL_WIDTH, MODEL_WIDTH), jnp.float32), (deltas, states))
    return weight_grad
```

```python
import jax
import jax.numpy as jnp
from jax import lax
from jax.sharding import PartitionSpec as P

MAXR = 3
EPS = 1e-06


def spread(block, axis, count):
    return lax.all_to_all(jnp.broadcast_to(block[None], (count,) + block.shape), axis, 0, 0)


def local(
    prelude_output, init_noise, core_weight, norm_gain, state_cotangent, step_counts, group_table
):
    local_width, full_width = core_weight.shape
    slot_total, seq_length = init_noise.shape[:2]
    rows = slot_total * seq_length
    mp_count = full_width // local_width
    dp_count = lax.axis_size("dp")
    my_group = lax.axis_index("dp")
    column_first = lax.axis_index("mp") * local_width
    seq_index = jnp.arange(group_table.shape[0], dtype=jnp.int32)

    noise = init_noise.reshape(rows, local_width).T
    first_state = spread(noise, "mp", mp_count).reshape(full_width, rows)

    earlier = (group_table[:, None] == group_table[None, :]) & (
        seq_index[None, :] < seq_index[:, None]
    )
    slot_rank = jnp.sum(earlier.astype(jnp.int32), axis=1)
    selected = (group_table[None, :] == my_group) & (
        slot_rank[None, :] == jnp.arange(slot_total, dtype=jnp.int32)[:, None]
    )
    slot_counts = jnp.sum(jnp.where(selected, step_counts[None, :], 0), axis=1)
    token_counts = jnp.repeat(slot_counts, seq_length)
    active = [(turn >= MAXR - token_counts)[None, :] for turn in range(MAXR)]
    inject = (
        jnp.einsum(
            "br,ref->bef",
            selected.astype(jnp.bfloat16),
            lax.all_gather(prelude_output, "dp", axis=0, tiled=True),
            preferred_element_type=jnp.float32,
        )
        .reshape(rows, local_width)
        .T
    )
    gain = norm_gain[:, None]
    gain_local = lax.dynamic_slice_in_dim(norm_gain, column_first, local_width, 0)[:, None]
    upstream = state_cotangent.reshape(rows, local_width).T.astype(jnp.float32)
    scaled = upstream * gain_local

    def project(state):
        return jnp.dot(core_weight, state, preferred_element_type=jnp.float32)

    states = [first_state]
    mixed_local, inverse_rms = [], []
    for turn in range(MAXR - 1):
        mixed = (project(states[turn]) + inject).astype(jnp.bfloat16)
        mixed_local.append(mixed.astype(jnp.float32))
        whole = spread(mixed, "mp", mp_count).reshape(full_width, rows).astype(jnp.float32)
        inverse = lax.rsqrt(jnp.sum(whole * whole, axis=0, keepdims=True) / full_width + EPS)
        inverse_rms.append(inverse)
        renewed = (gain * whole * inverse).astype(jnp.bfloat16)
        states.append(jnp.where(active[turn], renewed, states[turn]))

    product = project(states[2])
    last = (product + inject).astype(jnp.bfloat16).astype(jnp.float32)
    sums = jnp.stack(
        [
            jnp.sum(last * last, axis=0),
            jnp.sum(scaled * last, axis=0),
            jnp.sum(scaled * product, axis=0),
            jnp.sum(last * product, axis=0),
        ]
    )
    totals = jnp.sum(spread(sums, "mp", mp_count), axis=0)
    inverse_2 = lax.rsqrt(totals[0:1] / full_width + EPS)
    pull = inverse_2**3 * totals[1:2] / full_width
    delta_2 = jnp.where(active[2], inverse_2 * scaled - last * pull, 0.0).astype(jnp.bfloat16)

    inverse_1 = inverse_rms[1]
    inner_1 = (inverse_2 * totals[2:3] - pull * totals[3:4]) / inverse_1

    partial = lax.dot_general(
        core_weight, delta_2, (((0,), (0,)), ((), ())), preferred_element_type=jnp.float32
    ).astype(jnp.bfloat16)
    pieces = lax.all_to_all(partial.reshape(mp_count, local_width, rows), "mp", 0, 0)
    grad_in = jnp.sum(pieces.astype(jnp.float32), axis=0)
    delta_1 = jnp.where(
        active[1],
        inverse_1 * (grad_in * gain_local)
        - mixed_local[1] * (inverse_1**3 * inner_1 / full_width),
        0.0,
    ).astype(jnp.bfloat16)

    def outer(state, delta):
        return lax.dot_general(
            state, delta, (((1,), (1,)), ((), ())), preferred_element_type=jnp.float32
        )

    weight_grad = (outer(states[2], delta_2) + outer(states[1], delta_1)).astype(jnp.bfloat16)
    parts = lax.all_to_all(
        weight_grad.reshape(dp_count, full_width // dp_count, local_width), "dp", 0, 0
    )
    return jnp.sum(parts.astype(jnp.float32), axis=0).T


def solution(mesh):
    return jax.shard_map(
        local,
        mesh=mesh,
        in_specs=(
            P("dp", None, "mp"),
            P("dp", None, "mp"),
            P("mp", None),
            P(),
            P("dp", None, "mp"),
            P(),
            P(),
        ),
        out_specs=P("mp", "dp"),
        check_vma=False,
    )
```

```python
import jax
import jax.numpy as jnp
from jax import lax
from jax.sharding import Mesh, PartitionSpec as P

MAXR = 3
EPS = 1e-06
ZL, X, CORE, ZH, Y = 3, 4, 2, 4, 8
DP = ("zl", "x", "core")
MP = ("zh", "y")


def spread(block, axis, count):
    return lax.all_to_all(jnp.broadcast_to(block[None], (count,) + block.shape), axis, 0, 0)


def shift(value, axis, count, by):
    return lax.ppermute(value, axis, [(i, (i + by) % count) for i in range(count)])


def turned(array, axis):
    flipped = lax.rev(array, (axis,))
    double = lax.concatenate([flipped, flipped], axis)
    return lax.dynamic_slice_in_dim(double, ZH - 1 - lax.axis_index("zh"), ZH, axis)


def gather_features(block):
    bundle = jnp.stack([block] + [shift(block, "zh", ZH, by) for by in range(1, ZH)])
    return spread(bundle, "y", Y)


def scatter_features(partial):
    column = jnp.sum(lax.all_to_all(partial, "y", 0, 0).astype(jnp.float32), axis=0)
    total = column[0]
    for by in range(1, ZH):
        piece = column[by].astype(jnp.bfloat16)
        total = total + shift(piece, "zh", ZH, -by).astype(jnp.float32)
    return total


def local(
    prelude_output, init_noise, core_weight, norm_gain, state_cotangent, step_counts, group_table
):
    local_width, full_width = core_weight.shape
    slot_total, seq_length = init_noise.shape[:2]
    rows = slot_total * seq_length
    mp_count = ZH * Y
    dp_count = ZL * X * CORE
    padded = -(-local_width // 8) * 8
    extra = padded - local_width
    my_group = lax.axis_index(DP)
    column_first = lax.axis_index(MP) * local_width
    seq_index = jnp.arange(group_table.shape[0], dtype=jnp.int32)

    def columns(array):
        return jnp.pad(array.reshape(rows, local_width).T, ((0, extra), (0, 0)))

    first_state = gather_features(columns(init_noise))

    earlier = (group_table[:, None] == group_table[None, :]) & (
        seq_index[None, :] < seq_index[:, None]
    )
    slot_rank = jnp.sum(earlier.astype(jnp.int32), axis=1)
    selected = (group_table[None, :] == my_group) & (
        slot_rank[None, :] == jnp.arange(slot_total, dtype=jnp.int32)[:, None]
    )
    slot_counts = jnp.sum(jnp.where(selected, step_counts[None, :], 0), axis=1)
    token_counts = jnp.repeat(slot_counts, seq_length)
    active = [(turn >= MAXR - token_counts)[None, :] for turn in range(MAXR)]
    preludes = spread(prelude_output, DP, dp_count).reshape((-1,) + prelude_output.shape[1:])
    inject = columns(
        jnp.einsum(
            "br,ref->bef",
            selected.astype(jnp.bfloat16),
            preludes,
            preferred_element_type=jnp.float32,
        )
    )
    weight = jnp.pad(
        turned(core_weight.reshape(local_width, ZH, Y, local_width), 1).transpose(0, 2, 1, 3),
        ((0, extra), (0, 0), (0, 0), (0, extra)),
    ).reshape(padded, mp_count * padded)
    gain = jnp.pad(
        turned(norm_gain.reshape(ZH, Y, local_width), 0).transpose(1, 0, 2), ((0, 0), (0, 0), (0, extra))
    ).reshape(mp_count * padded, 1)
    gain_local = jnp.pad(
        lax.dynamic_slice_in_dim(norm_gain, column_first, local_width, 0), (0, extra)
    )[:, None]
    scaled = columns(state_cotangent).astype(jnp.float32) * gain_local

    def project(state):
        return jnp.dot(weight, state, preferred_element_type=jnp.float32)

    states = [first_state.reshape(mp_count * padded, rows)]
    mixed_local, inverse_rms = [], []
    for turn in range(MAXR - 1):
        mixed = (project(states[turn]) + inject).astype(jnp.bfloat16)
        mixed_local.append(mixed.astype(jnp.float32))
        whole = gather_features(mixed).reshape(mp_count * padded, rows).astype(jnp.float32)
        inverse = lax.rsqrt(jnp.sum(whole * whole, axis=0, keepdims=True) / full_width + EPS)
        inverse_rms.append(inverse)
        renewed = (gain * whole * inverse).astype(jnp.bfloat16)
        states.append(jnp.where(active[turn], renewed, states[turn]))

    product = project(states[2])
    last = (product + inject).astype(jnp.bfloat16).astype(jnp.float32)
    sums = jnp.stack(
        [
            jnp.sum(last * last, axis=0),
            jnp.sum(scaled * last, axis=0),
            jnp.sum(scaled * product, axis=0),
            jnp.sum(last * product, axis=0),
        ]
    )
    totals = jnp.sum(spread(sums, MP, mp_count), axis=0)
    inverse_2 = lax.rsqrt(totals[0:1] / full_width + EPS)
    pull = inverse_2**3 * totals[1:2] / full_width
    delta_2 = jnp.where(active[2], inverse_2 * scaled - last * pull, 0.0).astype(jnp.bfloat16)

    inverse_1 = inverse_rms[1]
    inner_1 = (inverse_2 * totals[2:3] - pull * totals[3:4]) / inverse_1

    partial = lax.dot_general(
        weight, delta_2, (((0,), (0,)), ((), ())), preferred_element_type=jnp.float32
    ).astype(jnp.bfloat16)
    grad_in = scatter_features(partial.reshape(Y, ZH, padded, rows))
    delta_1 = jnp.where(
        active[1],
        inverse_1 * (grad_in * gain_local)
        - mixed_local[1] * (inverse_1**3 * inner_1 / full_width),
        0.0,
    ).astype(jnp.bfloat16)

    def outer(state, delta):
        blocks = turned(state.reshape(Y, ZH, padded, rows), 1)[:, :, :local_width]
        blocks = blocks.transpose(1, 0, 2, 3).reshape(dp_count, full_width // dp_count, rows)
        return jnp.einsum(
            "dft,ot->dof", blocks, delta[:local_width], preferred_element_type=jnp.float32
        )

    weight_grad = outer(states[2], delta_2) + outer(states[1], delta_1)
    halves = weight_grad.reshape((ZL * X, CORE) + weight_grad.shape[1:])
    core = lax.axis_index("core")
    kept = lax.dynamic_index_in_dim(halves, core, 1, False)
    given = lax.dynamic_index_in_dim(halves, 1 - core, 1, False).astype(jnp.bfloat16)
    chip_sum = (kept + shift(given, "core", CORE, 1).astype(jnp.float32)).astype(jnp.bfloat16)
    parts = lax.all_to_all(chip_sum, ("zl", "x"), 0, 0)
    return jnp.sum(parts.astype(jnp.float32), axis=0)


def solution(mesh):
    fine = Mesh(mesh.devices.reshape(ZL, X, CORE, ZH, Y), ("zl", "x", "core", "zh", "y"))
    return jax.shard_map(
        local,
        mesh=fine,
        in_specs=(
            P(DP, None, MP),
            P(DP, None, MP),
            P(MP, None),
            P(),
            P(DP, None, MP),
            P(),
            P(),
        ),
        out_specs=P(MP, DP),
        check_vma=False,
    )
```

```python
import jax
import jax.numpy as jnp
from jax import lax
from jax.experimental import pallas as pl
from jax.experimental.pallas import tpu as pltpu
from jax.sharding import Mesh, PartitionSpec as P

MAXR = 3
EPS = 1e-06
ZL, X, CORE, ZH, Y = 3, 4, 2, 4, 8
DP = ("zl", "x", "core")
MP = ("zh", "y")


def spread(block, axis, count):
    return lax.all_to_all(jnp.broadcast_to(block[None], (count,) + block.shape), axis, 0, 0)


def shift(value, axis, count, by):
    return lax.ppermute(value, axis, [(i, (i + by) % count) for i in range(count)])


def turned(array, axis):
    flipped = lax.rev(array, (axis,))
    double = lax.concatenate([flipped, flipped], axis)
    return lax.dynamic_slice_in_dim(double, ZH - 1 - lax.axis_index("zh"), ZH, axis)


def weight_kernel(zh_ref, weight_ref, out_ref):
    zh = zh_ref[0]
    width = weight_ref.shape[0]
    out_ref[...] = jnp.zeros_like(out_ref)
    for index in range(ZH * Y):
        place = lax.rem(zh - index // Y + ZH, ZH)
        value = weight_ref[:, index * width : (index + 1) * width]
        out_ref[index % Y, place, :width, :width] = value


def arrange_weight(core_weight, padded):
    return pl.pallas_call(
        weight_kernel,
        out_shape=jax.ShapeDtypeStruct((Y, ZH, padded, padded), core_weight.dtype),
        in_specs=[pl.BlockSpec(memory_space=pltpu.SMEM), pl.BlockSpec(memory_space=pltpu.VMEM)],
        out_specs=pl.BlockSpec(memory_space=pltpu.VMEM),
    )(lax.axis_index("zh").astype(jnp.int32)[None], core_weight)


def bundle_features(block):
    return jnp.stack([block] + [shift(block, "zh", ZH, by) for by in range(1, ZH)])


def gather_features(block):
    return spread(bundle_features(block), "y", Y)


def scatter_features(partial):
    column = jnp.sum(lax.all_to_all(partial, "y", 0, 0).astype(jnp.float32), axis=0)
    total = column[0]
    for by in range(1, ZH):
        piece = column[by].astype(jnp.bfloat16)
        total = total + shift(piece, "zh", ZH, -by).astype(jnp.float32)
    return total


def local(
    prelude_output, init_noise, core_weight, norm_gain, state_cotangent, step_counts, group_table
):
    local_width, full_width = core_weight.shape
    slot_total, seq_length = init_noise.shape[:2]
    rows = slot_total * seq_length
    mp_count = ZH * Y
    dp_count = ZL * X * CORE
    padded = -(-local_width // 8) * 8
    extra = padded - local_width
    my_group = lax.axis_index(DP)
    column_first = lax.axis_index(MP) * local_width
    seq_index = jnp.arange(group_table.shape[0], dtype=jnp.int32)

    def columns(array):
        return jnp.pad(array.reshape(rows, local_width).T, ((0, extra), (0, 0)))

    bundle, later_prelude = lax.optimization_barrier(
        (bundle_features(columns(init_noise)), prelude_output)
    )
    first_state = spread(bundle, "y", Y)

    earlier = (group_table[:, None] == group_table[None, :]) & (
        seq_index[None, :] < seq_index[:, None]
    )
    slot_rank = jnp.sum(earlier.astype(jnp.int32), axis=1)
    selected = (group_table[None, :] == my_group) & (
        slot_rank[None, :] == jnp.arange(slot_total, dtype=jnp.int32)[:, None]
    )
    slot_counts = jnp.sum(jnp.where(selected, step_counts[None, :], 0), axis=1)
    token_counts = jnp.repeat(slot_counts, seq_length)
    active = [(turn >= MAXR - token_counts)[None, :] for turn in range(MAXR)]
    preludes = lax.all_gather(later_prelude, DP, axis=0, tiled=True)
    inject = columns(
        jnp.einsum(
            "br,ref->bef",
            selected.astype(jnp.bfloat16),
            preludes,
            preferred_element_type=jnp.float32,
        )
    )
    weight = arrange_weight(core_weight, padded)
    gain = jnp.pad(
        turned(norm_gain.reshape(ZH, Y, local_width), 0).transpose(1, 0, 2), ((0, 0), (0, 0), (0, extra))
    )
    gain_local = jnp.pad(
        lax.dynamic_slice_in_dim(norm_gain, column_first, local_width, 0), (0, extra)
    )[:, None]
    scaled = columns(state_cotangent).astype(jnp.float32) * gain_local

    def project(state):
        return jnp.einsum("yzok,yzkt->ot", weight, state, preferred_element_type=jnp.float32)

    first_state, inject, gain, gain_local, scaled, weight, active = lax.optimization_barrier(
        (first_state, inject, gain, gain_local, scaled, weight, active)
    )

    states = [first_state]
    mixed_local, inverse_rms = [], []
    for turn in range(MAXR - 1):
        mixed = (project(states[turn]) + inject).astype(jnp.bfloat16)
        mixed_local.append(mixed.astype(jnp.float32))
        whole = gather_features(mixed).astype(jnp.float32)
        inverse = lax.rsqrt(jnp.sum(whole * whole, axis=(0, 1, 2))[None] / full_width + EPS)
        inverse_rms.append(inverse)
        renewed = (gain[..., None] * whole * inverse).astype(jnp.bfloat16)
        states.append(jnp.where(active[turn], renewed, states[turn]))

    product = project(states[2])
    last = (product + inject).astype(jnp.bfloat16).astype(jnp.float32)
    sums = jnp.stack(
        [
            jnp.sum(last * last, axis=0),
            jnp.sum(scaled * last, axis=0),
            jnp.sum(scaled * product, axis=0),
            jnp.sum(last * product, axis=0),
        ]
    )
    totals = jnp.sum(spread(sums, MP, mp_count), axis=0)
    inverse_2 = lax.rsqrt(totals[0:1] / full_width + EPS)
    pull = inverse_2**3 * totals[1:2] / full_width
    delta_2 = jnp.where(active[2], inverse_2 * scaled - last * pull, 0.0).astype(jnp.bfloat16)

    inverse_1 = inverse_rms[1]
    inner_1 = (inverse_2 * totals[2:3] - pull * totals[3:4]) / inverse_1

    partial = jnp.einsum("yzok,ot->yzkt", weight, delta_2, preferred_element_type=jnp.float32)
    grad_in = scatter_features(partial.astype(jnp.bfloat16))
    delta_1 = jnp.where(
        active[1],
        inverse_1 * (grad_in * gain_local)
        - mixed_local[1] * (inverse_1**3 * inner_1 / full_width),
        0.0,
    ).astype(jnp.bfloat16)

    def outer(state, delta):
        blocks = turned(state, 1)[:, :, :local_width]
        blocks = blocks.transpose(1, 0, 2, 3).reshape(dp_count, full_width // dp_count, rows)
        return jnp.einsum(
            "dft,ot->dof", blocks, delta[:local_width], preferred_element_type=jnp.float32
        )

    weight_grad = outer(states[2], delta_2) + outer(states[1], delta_1)
    halves = weight_grad.reshape((ZL * X, CORE) + weight_grad.shape[1:])
    core = lax.axis_index("core")
    kept = lax.dynamic_index_in_dim(halves, core, 1, False)
    given = lax.dynamic_index_in_dim(halves, 1 - core, 1, False).astype(jnp.bfloat16)
    chip_sum = (kept + shift(given, "core", CORE, 1).astype(jnp.float32)).astype(jnp.bfloat16)
    parts = lax.all_to_all(chip_sum, ("zl", "x"), 0, 0)
    return jnp.sum(parts.astype(jnp.float32), axis=0)


def solution(mesh):
    fine = Mesh(mesh.devices.reshape(ZL, X, CORE, ZH, Y), ("zl", "x", "core", "zh", "y"))
    return jax.shard_map(
        local,
        mesh=fine,
        in_specs=(
            P(DP, None, MP),
            P(DP, None, MP),
            P(MP, None),
            P(),
            P(DP, None, MP),
            P(),
            P(),
        ),
        out_specs=P(MP, DP),
        check_vma=False,
    )
```

```python
import jax
import jax.numpy as jnp
from jax import lax
from jax.experimental import pallas as pl
from jax.experimental.pallas import tpu as pltpu
from jax.sharding import Mesh, PartitionSpec as P

MAXR = 3
EPS = 1e-06
ZL, X, CORE, ZH, Y = 3, 4, 2, 4, 8
DP = ("zl", "x", "core")
MP = ("zh", "y")
PIECES = 3
BF16, F32 = jnp.bfloat16, jnp.float32


def spread(block, axis, count):
    return lax.all_to_all(jnp.broadcast_to(block[None], (count,) + block.shape), axis, 0, 0)


def shift(value, axis, count, by):
    return lax.ppermute(value, axis, [(i, (i + by) % count) for i in range(count)])


def turned(array, axis):
    flipped = lax.rev(array, (axis,))
    double = lax.concatenate([flipped, flipped], axis)
    return lax.dynamic_slice_in_dim(double, ZH - 1 - lax.axis_index("zh"), ZH, axis)


def weight_kernel(zh_ref, weight_ref, out_ref):
    zh = zh_ref[0]
    width = weight_ref.shape[0]
    out_ref[...] = jnp.zeros_like(out_ref)
    for index in range(ZH * Y):
        place = lax.rem(zh - index // Y + ZH, ZH)
        value = weight_ref[:, index * width : (index + 1) * width]
        out_ref[index % Y, place, :width, :width] = value


def arrange_weight(core_weight, padded):
    return pl.pallas_call(
        weight_kernel,
        out_shape=jax.ShapeDtypeStruct((Y, ZH, padded, padded), core_weight.dtype),
        in_specs=[pl.BlockSpec(memory_space=pltpu.SMEM), pl.BlockSpec(memory_space=pltpu.VMEM)],
        out_specs=pl.BlockSpec(memory_space=pltpu.VMEM),
    )(lax.axis_index("zh").astype(jnp.int32)[None], core_weight)


def gather_z(block):
    return jnp.stack([block] + [shift(block, "zh", ZH, by) for by in range(1, ZH)])


def to_pieces(sums):
    pieces = []
    for _ in range(PIECES):
        piece = lax.reduce_precision(sums, 8, 7)
        pieces.append(piece.astype(BF16))
        sums = sums - piece
    return jnp.concatenate(pieces)


def from_pieces(rows):
    rows = jnp.sum(rows, axis=tuple(range(rows.ndim - 2)))
    return jnp.sum(rows.reshape(PIECES, -1, rows.shape[-1]), axis=0)


def local(
    prelude_output, init_noise, core_weight, norm_gain, state_cotangent, step_counts, group_table
):
    width, full_width = core_weight.shape
    slot_total, seq_length = init_noise.shape[:2]
    rows = slot_total * seq_length
    dp_count = ZL * X * CORE
    padded = -(-width // 8) * 8
    extra = padded - width
    my_group = lax.axis_index(DP)
    column_first = lax.axis_index(MP) * width
    seq_index = jnp.arange(group_table.shape[0], dtype=jnp.int32)
    real = (jnp.arange(padded) < width)[:, None]

    def columns(array):
        return jnp.pad(array.reshape(rows, width).T, ((0, extra), (0, 0)))

    arranged = arrange_weight(core_weight, padded)
    arranged, noise, prelude, cotangent = lax.optimization_barrier(
        (arranged, init_noise, prelude_output, state_cotangent)
    )
    weight = lax.all_to_all(arranged, "y", 0, 0)
    first_state = gather_z(columns(noise))

    earlier = (group_table[:, None] == group_table[None, :]) & (
        seq_index[None, :] < seq_index[:, None]
    )
    slot_rank = jnp.sum(earlier.astype(jnp.int32), axis=1)
    selected = (group_table[None, :] == my_group) & (
        slot_rank[None, :] == jnp.arange(slot_total, dtype=jnp.int32)[:, None]
    )
    slot_counts = jnp.sum(jnp.where(selected, step_counts[None, :], 0), axis=1)
    token_counts = jnp.repeat(slot_counts, seq_length)
    active = [(turn >= MAXR - token_counts)[None, :] for turn in range(MAXR)]
    inject = columns(
        jnp.einsum(
            "br,ref->bef",
            selected.astype(BF16),
            lax.all_gather(prelude, DP, axis=0, tiled=True),
            preferred_element_type=F32,
        )
    )
    own_gains = turned(norm_gain.reshape(ZH, Y, width), 0)
    gains = jnp.pad(
        lax.dynamic_index_in_dim(own_gains, lax.axis_index("y"), 1, False), ((0, 0), (0, extra))
    )
    gain_local = jnp.pad(
        lax.dynamic_slice_in_dim(norm_gain, column_first, width, 0), (0, extra)
    )[:, None]
    scaled = columns(cotangent).astype(F32) * gain_local

    first_state, weight, inject, gains, gain_local, scaled, active = lax.optimization_barrier(
        (first_state, weight, inject, gains, gain_local, scaled, active)
    )

    def project(state, squares):
        partial = jnp.einsum("yzok,zkt->yot", weight, state, preferred_element_type=F32)
        partial = partial.astype(BF16)
        if squares is None:
            pull = jnp.broadcast_to(scaled.astype(BF16)[None], partial.shape)
            both = lax.all_to_all(jnp.concatenate([partial, pull], axis=1), "y", 0, 0)
            return jnp.sum(both[:, :padded].astype(F32), axis=0), both[:, padded:]
        spare = jnp.broadcast_to(to_pieces(squares)[None], (Y, PIECES, rows))
        partial = jnp.concatenate([partial[:, :width], spare], axis=1)
        parts = lax.all_to_all(partial, "y", 0, 0).astype(F32)
        return jnp.sum(jnp.where(real, parts, 0.0), axis=0), parts[:, width:]

    states, factors, inverse_rms, mixed_local = [first_state], [None], [], []
    squares = None
    for turn in range(MAXR):
        product, spare = project(states[turn], squares)
        if not turn:
            pulled = spare
        else:
            inverse = lax.rsqrt(from_pieces(spare) / full_width + EPS)
            inverse_rms.append(inverse)
            factors.append(jnp.where(active[turn - 1], inverse, 1.0))
            product = product * factors[turn]
        mixed = (product + inject).astype(BF16)
        mixed_local.append(mixed.astype(F32))
        if turn + 1 < MAXR:
            whole = gather_z(mixed).astype(F32)
            squares = jnp.sum(whole * whole, axis=(0, 1))[None]
            renewed = (gains[:, :, None] * whole).astype(BF16)
            states.append(jnp.where(active[turn][None], renewed, states[turn]))

    last = mixed_local[2]
    sums = jnp.stack(
        [
            jnp.sum(last * last, axis=0),
            jnp.sum(scaled * last, axis=0),
            jnp.sum(scaled * product, axis=0),
            jnp.sum(last * product, axis=0),
        ]
    )
    sent = jnp.concatenate([mixed, to_pieces(sums)])
    along = spread(sent, "y", Y)

    def transposed(values):
        part = jnp.einsum("yzok,yot->zkt", weight, values, preferred_element_type=F32)
        return part.astype(BF16)

    column_sums = to_pieces(from_pieces(along[:, padded:].astype(F32)))
    column_sums = jnp.broadcast_to(column_sums[None], (ZH,) + column_sums.shape)
    partial = jnp.concatenate([transposed(along[:, :padded]), transposed(pulled), column_sums], 1)
    arrived = jnp.stack(
        [partial[0]] + [shift(partial[by], "zh", ZH, -by) for by in range(1, ZH)]
    ).astype(F32)
    through_last = jnp.sum(arrived[:, :padded], axis=0)
    through_scaled = jnp.sum(arrived[:, padded : 2 * padded], axis=0)
    totals = from_pieces(arrived[:, 2 * padded :])

    inverse_2 = lax.rsqrt(totals[0:1] / full_width + EPS)
    pull = inverse_2**3 * totals[1:2] / full_width
    delta_2 = jnp.where(active[2], inverse_2 * scaled - last * pull, 0.0)
    grad_in = inverse_2 * through_scaled - pull * through_last
    inverse_1 = inverse_rms[1]
    inner_1 = (inverse_2 * totals[2:3] - pull * totals[3:4]) / inverse_1
    delta_1 = jnp.where(
        active[1],
        inverse_1 * (grad_in * gain_local)
        - mixed_local[1] * (inverse_1**3 * inner_1 / full_width),
        0.0,
    )

    def outer(state, delta):
        whole = turned(lax.all_gather(state, "y", axis=0), 1)[:, :, :width]
        blocks = whole.transpose(1, 0, 2, 3).reshape(dp_count, full_width // dp_count, rows)
        return jnp.einsum(
            "dft,ot->dof", blocks, delta[:width].astype(BF16), preferred_element_type=F32
        )

    weight_grad = outer(states[2], delta_2 * factors[2]) + outer(states[1], delta_1 * factors[1])
    halves = weight_grad.reshape((ZL * X, CORE) + weight_grad.shape[1:])
    core = lax.axis_index("core")
    kept = lax.dynamic_index_in_dim(halves, core, 1, False)
    given = lax.dynamic_index_in_dim(halves, 1 - core, 1, False).astype(BF16)
    chip_sum = (kept + shift(given, "core", CORE, 1).astype(F32)).astype(BF16)
    parts = lax.all_to_all(chip_sum, ("zl", "x"), 0, 0)
    return jnp.sum(parts.astype(F32), axis=0)


def solution(mesh):
    fine = Mesh(mesh.devices.reshape(ZL, X, CORE, ZH, Y), ("zl", "x", "core", "zh", "y"))
    return jax.shard_map(
        local,
        mesh=fine,
        in_specs=(
            P(DP, None, MP),
            P(DP, None, MP),
            P(MP, None),
            P(),
            P(DP, None, MP),
            P(),
            P(),
        ),
        out_specs=P(MP, DP),
        check_vma=False,
    )
```

```python
import jax
import jax.numpy as jnp
from jax import lax
from jax.experimental import pallas as pl
from jax.experimental.pallas import tpu as pltpu
from jax.sharding import Mesh, PartitionSpec as P

MAXR = 3
EPS = 1e-06
ZL, X, CORE, ZH, Y = 3, 4, 2, 4, 8
DP = ("zl", "x", "core")
MP = ("zh", "y")
PIECES = 3
LANES = 128
BF16, F32 = jnp.bfloat16, jnp.float32


def spread(block, axis, count):
    return lax.all_to_all(jnp.broadcast_to(block[None], (count,) + block.shape), axis, 0, 0)


def shift(value, axis, count, by):
    return lax.ppermute(value, axis, [(i, (i + by) % count) for i in range(count)])


def turned(array, axis):
    flipped = lax.rev(array, (axis,))
    double = lax.concatenate([flipped, flipped], axis)
    return lax.dynamic_slice_in_dim(double, ZH - 1 - lax.axis_index("zh"), ZH, axis)


def pack_kernel(zh_ref, weight_ref, pull_ref, out_ref):
    zh = zh_ref[0]
    width, padded = weight_ref.shape[0], pull_ref.shape[0]
    third = padded // 3
    lanes = padded - LANES
    out_ref[...] = jnp.zeros_like(out_ref)
    for index in range(ZH * Y):
        first = index * width
        place = lax.rem(zh - index // Y + ZH, ZH)
        out_ref[index % Y, place, :width, :] = weight_ref[:, first : first + LANES]
        for fold in range(3):
            low, high = fold * third, min(fold * third + third, width)
            out_ref[
                index % Y, place, padded : padded + high - low,
                fold * lanes : fold * lanes + width - LANES,
            ] = weight_ref[low:high, first + LANES : first + width]
    for index in range(Y):
        out_ref[index, ZH, :padded, :] = pull_ref[...]


def unpack_kernel(packed_ref, out_ref):
    padded = out_ref.shape[-1]
    third = padded // 3
    lanes = padded - LANES
    for y in range(Y):
        for s in range(ZH):
            out_ref[y, s, :, :LANES] = packed_ref[y, s, :padded, :]
            for fold in range(3):
                out_ref[y, s, fold * third : fold * third + third, LANES:] = packed_ref[
                    y, s, padded : padded + third, fold * lanes : fold * lanes + lanes
                ]


def grad_kernel(place_ref, state_1, delta_1, state_2, delta_2, kept_ref, given_ref, flat_1, flat_2):
    zh, core = place_ref[0], place_ref[1]
    width, piece = kept_ref.shape[1:]
    for part in range(ZH):
        place = lax.rem(zh - part + ZH, ZH)
        for state, flat in ((state_1, flat_1), (state_2, flat_2)):
            for y in range(Y):
                flat[y * width : y * width + width, :] = state[y, place][:width].astype(F32)
        for block in range(Y * width // piece):
            group = part * (Y * width // piece) + block
            value = 0.0
            for flat, delta in ((flat_1, delta_1), (flat_2, delta_2)):
                value = value + lax.dot_general(
                    delta[...],
                    flat[block * piece : block * piece + piece, :].astype(BF16),
                    (((1,), (1,)), ((), ())),
                    preferred_element_type=F32,
                )
            value = value[:width].astype(BF16)

            @pl.when(core == group % CORE)
            def _():
                kept_ref[group // CORE] = value

            @pl.when(core != group % CORE)
            def _():
                given_ref[group // CORE] = value


IN_VMEM = pl.BlockSpec(memory_space=pltpu.VMEM)
IN_SMEM = pl.BlockSpec(memory_space=pltpu.SMEM)


def position(name):
    return lax.axis_index(name).astype(jnp.int32)


def gather_z(block):
    return jnp.stack([block] + [shift(block, "zh", ZH, by) for by in range(1, ZH)])


def to_pieces(sums):
    pieces = []
    for _ in range(PIECES):
        piece = lax.reduce_precision(sums, 8, 7)
        pieces.append(piece.astype(BF16))
        sums = sums - piece
    return jnp.concatenate(pieces)


def from_pieces(rows):
    rows = jnp.sum(rows, axis=tuple(range(rows.ndim - 2)))
    return jnp.sum(rows.reshape(PIECES, -1, rows.shape[-1]), axis=0)


def local(
    prelude_output, init_noise, core_weight, norm_gain, state_cotangent, step_counts, group_table
):
    width, full_width = core_weight.shape
    slot_total, seq_length = init_noise.shape[:2]
    rows = slot_total * seq_length
    dp_count = ZL * X * CORE
    padded = -(-width // 8) * 8
    extra = padded - width
    my_group = lax.axis_index(DP)
    column_first = lax.axis_index(MP) * width
    seq_index = jnp.arange(group_table.shape[0], dtype=jnp.int32)
    real = (jnp.arange(padded) < width)[:, None]

    def columns(array):
        return jnp.pad(array.reshape(rows, width).T, ((0, extra), (0, 0)))

    gain_local = jnp.pad(
        lax.dynamic_slice_in_dim(norm_gain, column_first, width, 0), (0, extra)
    )[:, None]
    scaled = columns(state_cotangent).astype(F32) * gain_local

    packed = pl.pallas_call(
        pack_kernel,
        out_shape=jax.ShapeDtypeStruct((Y, ZH + 1, padded + padded // 3, LANES), BF16),
        in_specs=[IN_SMEM, IN_VMEM, IN_VMEM],
        out_specs=IN_VMEM,
    )(position("zh")[None], core_weight, scaled.astype(BF16))
    packed, noise, prelude = lax.optimization_barrier((packed, init_noise, prelude_output))
    packed = lax.all_to_all(packed, "y", 0, 0)
    weight = pl.pallas_call(
        unpack_kernel,
        out_shape=jax.ShapeDtypeStruct((Y, ZH, padded, padded), BF16),
        in_specs=[IN_VMEM],
        out_specs=IN_VMEM,
    )(packed)
    pulled = packed[:, ZH, :padded]
    first_state = gather_z(columns(noise))

    earlier = (group_table[:, None] == group_table[None, :]) & (
        seq_index[None, :] < seq_index[:, None]
    )
    slot_rank = jnp.sum(earlier.astype(jnp.int32), axis=1)
    selected = (group_table[None, :] == my_group) & (
        slot_rank[None, :] == jnp.arange(slot_total, dtype=jnp.int32)[:, None]
    )
    slot_counts = jnp.sum(jnp.where(selected, step_counts[None, :], 0), axis=1)
    token_counts = jnp.repeat(slot_counts, seq_length)
    active = [(turn >= MAXR - token_counts)[None, :] for turn in range(MAXR)]
    both = jnp.stack([prelude, shift(prelude, "core", CORE, 1)])
    gathered = lax.all_gather(both, ("zl", "x"), axis=0)
    chosen = selected.astype(BF16).reshape(slot_total, ZL * X, CORE, -1)
    chosen = jnp.where(lax.axis_index("core") == 0, chosen, lax.rev(chosen, (2,)))
    inject = columns(
        jnp.einsum("bpcr,pcref->bef", chosen, gathered, preferred_element_type=F32)
    )
    own_gains = turned(norm_gain.reshape(ZH, Y, width), 0)
    gains = jnp.pad(
        lax.dynamic_index_in_dim(own_gains, lax.axis_index("y"), 1, False), ((0, 0), (0, extra))
    )
    first_state, weight, inject, gains, gain_local, scaled, active = lax.optimization_barrier(
        (first_state, weight, inject, gains, gain_local, scaled, active)
    )

    def project(state, squares):
        partial = jnp.einsum("yzok,zkt->yot", weight, state, preferred_element_type=F32)
        partial = partial.astype(BF16)
        if squares is None:
            return jnp.sum(lax.all_to_all(partial, "y", 0, 0).astype(F32), axis=0), None
        spare = jnp.broadcast_to(to_pieces(squares)[None], (Y, PIECES, rows))
        partial = jnp.concatenate([partial[:, :width], spare], axis=1)
        parts = lax.all_to_all(partial, "y", 0, 0).astype(F32)
        return jnp.sum(jnp.where(real, parts, 0.0), axis=0), parts[:, width:]

    states, factors, inverse_rms, mixed_local = [first_state], [None], [], []
    squares = None
    for turn in range(MAXR):
        product, spare = project(states[turn], squares)
        if turn:
            inverse = lax.rsqrt(from_pieces(spare) / full_width + EPS)
            inverse_rms.append(inverse)
            factors.append(jnp.where(active[turn - 1], inverse, 1.0))
            product = product * factors[turn]
        mixed = (product + inject).astype(BF16)
        mixed_local.append(mixed.astype(F32))
        if turn + 1 < MAXR:
            whole = gather_z(mixed).astype(F32)
            squares = jnp.sum(whole * whole, axis=(0, 1))[None]
            renewed = (gains[:, :, None] * whole).astype(BF16)
            states.append(jnp.where(active[turn][None], renewed, states[turn]))

    last = mixed_local[2]
    sums = jnp.stack(
        [
            jnp.sum(last * last, axis=0),
            jnp.sum(scaled * last, axis=0),
            jnp.sum(scaled * product, axis=0),
            jnp.sum(last * product, axis=0),
        ]
    )
    sent = jnp.concatenate([mixed, to_pieces(sums)])
    along = spread(sent, "y", Y)

    def transposed(values):
        part = jnp.einsum("yzok,yot->zkt", weight, values, preferred_element_type=F32)
        return part.astype(BF16)

    column_sums = to_pieces(from_pieces(along[:, padded:].astype(F32)))
    column_sums = jnp.broadcast_to(column_sums[None], (ZH,) + column_sums.shape)
    partial = jnp.concatenate([transposed(along[:, :padded]), transposed(pulled), column_sums], 1)
    arrived = jnp.stack(
        [partial[0]] + [shift(partial[by], "zh", ZH, -by) for by in range(1, ZH)]
    ).astype(F32)
    through_last = jnp.sum(arrived[:, :padded], axis=0)
    through_scaled = jnp.sum(arrived[:, padded : 2 * padded], axis=0)
    totals = from_pieces(arrived[:, 2 * padded :])

    inverse_2 = lax.rsqrt(totals[0:1] / full_width + EPS)
    pull = inverse_2**3 * totals[1:2] / full_width
    delta_2 = jnp.where(active[2], inverse_2 * scaled - last * pull, 0.0)
    grad_in = inverse_2 * through_scaled - pull * through_last
    inverse_1 = inverse_rms[1]
    inner_1 = (inverse_2 * totals[2:3] - pull * totals[3:4]) / inverse_1
    delta_1 = jnp.where(
        active[1],
        inverse_1 * (grad_in * gain_local)
        - mixed_local[1] * (inverse_1**3 * inner_1 / full_width),
        0.0,
    )

    half = jax.ShapeDtypeStruct((ZL * X, width, full_width // dp_count), BF16)
    kept, given = pl.pallas_call(
        grad_kernel,
        out_shape=(half, half),
        in_specs=[IN_SMEM] + [IN_VMEM] * 4,
        out_specs=(IN_VMEM, IN_VMEM),
        scratch_shapes=[pltpu.VMEM((Y * width, rows), F32)] * 2,
    )(
        jnp.stack([position("zh"), position("core")]),
        lax.all_gather(states[1], "y", axis=0),
        (delta_1 * factors[1]).astype(BF16),
        lax.all_gather(states[2], "y", axis=0),
        (delta_2 * factors[2]).astype(BF16),
    )
    chip_sum = (kept.astype(F32) + shift(given, "core", CORE, 1).astype(F32)).astype(BF16)
    parts = lax.all_to_all(chip_sum, ("zl", "x"), 0, 0)
    return jnp.sum(parts.astype(F32), axis=0)


def solution(mesh):
    fine = Mesh(mesh.devices.reshape(ZL, X, CORE, ZH, Y), ("zl", "x", "core", "zh", "y"))
    return jax.shard_map(
        local,
        mesh=fine,
        in_specs=(
            P(DP, None, MP),
            P(DP, None, MP),
            P(MP, None),
            P(),
            P(DP, None, MP),
            P(),
            P(),
        ),
        out_specs=P(MP, DP),
        check_vma=False,
    )
```

```python
import jax
import jax.numpy as jnp
from jax import lax
from jax.experimental import pallas as pl
from jax.experimental.layout import Layout, with_layout_constraint
from jax.experimental.pallas import tpu as pltpu
from jax.sharding import Mesh, PartitionSpec as P

MAXR = 3
EPS = 1e-06
ZL, X, CORE, ZH, Y = 3, 4, 2, 4, 8
DP = ("zl", "x", "core")
MP = ("zh", "y")
PIECES = 3
LANES = 128
BF16, F32 = jnp.bfloat16, jnp.float32


def spread(block, axis, count):
    return lax.all_to_all(jnp.broadcast_to(block[None], (count,) + block.shape), axis, 0, 0)


def shift(value, axis, count, by):
    return lax.ppermute(value, axis, [(i, (i + by) % count) for i in range(count)])


def turned(array, axis):
    flipped = lax.rev(array, (axis,))
    double = lax.concatenate([flipped, flipped], axis)
    return lax.dynamic_slice_in_dim(double, ZH - 1 - lax.axis_index("zh"), ZH, axis)


def pack_kernel(weight_ref, pull_ref, out_ref):
    width, padded = weight_ref.shape[0], pull_ref.shape[0]
    third = padded // 3
    lanes = padded - LANES
    out_ref[...] = jnp.zeros_like(out_ref)
    for index in range(ZH * Y):
        first = index * width
        place = index // Y
        out_ref[index % Y, place, :width, :] = weight_ref[:, first : first + LANES]
        for fold in range(3):
            low, high = fold * third, min(fold * third + third, width)
            out_ref[
                index % Y, place, padded : padded + high - low,
                fold * lanes : fold * lanes + width - LANES,
            ] = weight_ref[low:high, first + LANES : first + width]
    for index in range(Y):
        out_ref[index, ZH, :padded, :] = pull_ref[...]


def unpack_kernel(packed_ref, out_ref):
    padded = out_ref.shape[-1]
    third = padded // 3
    lanes = padded - LANES
    for y in range(Y):
        for s in range(ZH):
            out_ref[y, s, :, :LANES] = packed_ref[y, s, :padded, :]
            for fold in range(3):
                out_ref[y, s, fold * third : fold * third + third, LANES:] = packed_ref[
                    y, s, padded : padded + third, fold * lanes : fold * lanes + lanes
                ]


def grad_kernel(core_ref, state_1, state_2, delta_ref, kept_ref, given_ref, flat):
    core = core_ref[0]
    width, piece = kept_ref.shape[1:]
    rows = state_1.shape[-1]
    delta = delta_ref[...]
    for part in range(ZH):
        for step, state in enumerate((state_1, state_2)):
            for y in range(Y):
                flat[y * width : y * width + width, step * rows : step * rows + rows] = state[
                    y, part
                ][:width].astype(F32)
        for block in range(Y * width // piece):
            group = part * (Y * width // piece) + block
            value = lax.dot_general(
                delta,
                flat[block * piece : block * piece + piece, :].astype(BF16),
                (((1,), (1,)), ((), ())),
                preferred_element_type=F32,
            )
            value = value[:width].astype(BF16)

            @pl.when(core == group % CORE)
            def _():
                kept_ref[group // CORE] = value

            @pl.when(core != group % CORE)
            def _():
                given_ref[group // CORE] = value


IN_VMEM = pl.BlockSpec(memory_space=pltpu.VMEM)
IN_SMEM = pl.BlockSpec(memory_space=pltpu.SMEM)


def rotations(block, axis, count):
    return jnp.stack([block] + [shift(block, axis, count, by) for by in range(1, count)])


def to_pieces(sums):
    pieces = []
    for _ in range(PIECES):
        piece = lax.reduce_precision(sums, 8, 7)
        pieces.append(piece.astype(BF16))
        sums = sums - piece
    return jnp.concatenate(pieces)


def from_pieces(rows):
    rows = jnp.sum(rows, axis=tuple(range(rows.ndim - 2)))
    return jnp.sum(rows.reshape(PIECES, -1, rows.shape[-1]), axis=0)


def local(
    prelude_output, init_noise, core_weight, norm_gain, state_cotangent, step_counts, group_table
):
    width, full_width = core_weight.shape
    slot_total, seq_length = init_noise.shape[:2]
    rows = slot_total * seq_length
    dp_count = ZL * X * CORE
    padded = -(-width // 8) * 8
    extra = padded - width
    my_group = lax.axis_index(DP)
    column_first = lax.axis_index(MP) * width
    seq_index = jnp.arange(group_table.shape[0], dtype=jnp.int32)
    real = (jnp.arange(padded) < width)[:, None]

    def columns(array):
        return jnp.pad(array.reshape(rows, width).T, ((0, extra), (0, 0)))

    gain_local = jnp.pad(
        lax.dynamic_slice_in_dim(norm_gain, column_first, width, 0), (0, extra)
    )[:, None]
    scaled = columns(state_cotangent).astype(F32) * gain_local

    packed = pl.pallas_call(
        pack_kernel,
        out_shape=jax.ShapeDtypeStruct((Y, ZH + 1, padded + padded // 3, LANES), BF16),
        in_specs=[IN_VMEM, IN_VMEM],
        out_specs=IN_VMEM,
    )(core_weight, scaled.astype(BF16))
    packed, noise, prelude = lax.optimization_barrier((packed, init_noise, prelude_output))
    packed = lax.all_to_all(packed, "y", 0, 0)
    weight = pl.pallas_call(
        unpack_kernel,
        out_shape=jax.ShapeDtypeStruct((Y, ZH, padded, padded), BF16),
        in_specs=[IN_VMEM],
        out_specs=IN_VMEM,
    )(packed)
    pulled = packed[:, ZH, :padded]
    noise = with_layout_constraint(columns(noise), Layout((0, 1)))
    first_state = turned(rotations(noise, "zh", ZH), 0)
    first_state = with_layout_constraint(first_state, Layout((0, 1, 2)))

    earlier = (group_table[:, None] == group_table[None, :]) & (
        seq_index[None, :] < seq_index[:, None]
    )
    slot_rank = jnp.sum(earlier.astype(jnp.int32), axis=1)
    selected = (group_table[None, :] == my_group) & (
        slot_rank[None, :] == jnp.arange(slot_total, dtype=jnp.int32)[:, None]
    )
    slot_counts = jnp.sum(jnp.where(selected, step_counts[None, :], 0), axis=1)
    token_counts = jnp.repeat(slot_counts, seq_length)
    active = [(turn >= MAXR - token_counts)[None, :] for turn in range(MAXR)]
    gathered = rotations(rotations(rotations(prelude, "zl", ZL), "x", X), "core", CORE)
    home = seq_index // prelude.shape[0]
    distance = (lax.axis_index("core") - home + CORE) % CORE
    distance = distance * X + (lax.axis_index("x") - home // CORE % X + X) % X
    distance = distance * ZL + (lax.axis_index("zl") - home // (CORE * X) + ZL) % ZL
    arrival = distance * prelude.shape[0] + seq_index % prelude.shape[0]
    chosen = jnp.dot(
        selected.astype(BF16),
        (arrival[:, None] == seq_index[None, :]).astype(BF16),
        preferred_element_type=F32,
    ).astype(BF16)
    inject = columns(
        jnp.einsum(
            "br,ref->bef",
            chosen,
            gathered.reshape((-1,) + prelude.shape[1:]),
            preferred_element_type=F32,
        )
    )
    own_gains = norm_gain.reshape(ZH, Y, width)
    gains = jnp.pad(
        lax.dynamic_index_in_dim(own_gains, lax.axis_index("y"), 1, False), ((0, 0), (0, extra))
    )
    first_state, weight, inject, gains, gain_local, scaled, active = lax.optimization_barrier(
        (first_state, weight, inject, gains, gain_local, scaled, active)
    )

    def project(state, squares):
        partial = jnp.einsum("yzok,zkt->yot", weight, state, preferred_element_type=F32)
        partial = partial.astype(BF16)
        if squares is None:
            return jnp.sum(lax.all_to_all(partial, "y", 0, 0).astype(F32), axis=0), None
        spare = jnp.broadcast_to(to_pieces(squares)[None], (Y, PIECES, rows))
        partial = jnp.concatenate([partial[:, :width], spare], axis=1)
        parts = lax.all_to_all(partial, "y", 0, 0).astype(F32)
        return jnp.sum(jnp.where(real, parts, 0.0), axis=0), parts[:, width:]

    states, factors, inverse_rms, mixed_local = [first_state], [None], [], []
    squares = None
    for turn in range(MAXR):
        product, spare = project(states[turn], squares)
        if turn:
            inverse = lax.rsqrt(from_pieces(spare) / full_width + EPS)
            inverse_rms.append(inverse)
            factors.append(jnp.where(active[turn - 1], inverse, 1.0))
            product = product * factors[turn]
        mixed = (product + inject).astype(BF16)
        mixed_local.append(mixed.astype(F32))
        if turn + 1 < MAXR:
            whole = spread(mixed, "zh", ZH).astype(F32)
            squares = jnp.sum(whole * whole, axis=(0, 1))[None]
            renewed = (gains[:, :, None] * whole).astype(BF16)
            states.append(jnp.where(active[turn][None], renewed, states[turn]))

    last = mixed_local[2]
    sums = jnp.stack(
        [
            jnp.sum(last * last, axis=0),
            jnp.sum(scaled * last, axis=0),
            jnp.sum(scaled * product, axis=0),
            jnp.sum(last * product, axis=0),
        ]
    )
    sent = jnp.concatenate([mixed, to_pieces(sums)])
    along = spread(sent, "y", Y)

    def transposed(values):
        part = jnp.einsum("yzok,yot->zkt", weight, values, preferred_element_type=F32)
        return part.astype(BF16)

    column_sums = to_pieces(from_pieces(along[:, padded:].astype(F32)))
    column_sums = jnp.broadcast_to(column_sums[None], (ZH,) + column_sums.shape)
    partial = jnp.concatenate([transposed(along[:, :padded]), transposed(pulled), column_sums], 1)
    arrived = lax.all_to_all(partial, "zh", 0, 0).astype(F32)
    through_last = jnp.sum(arrived[:, :padded], axis=0)
    through_scaled = jnp.sum(arrived[:, padded : 2 * padded], axis=0)
    totals = from_pieces(arrived[:, 2 * padded :])

    inverse_2 = lax.rsqrt(totals[0:1] / full_width + EPS)
    pull = inverse_2**3 * totals[1:2] / full_width
    delta_2 = jnp.where(active[2], inverse_2 * scaled - last * pull, 0.0)
    grad_in = inverse_2 * through_scaled - pull * through_last
    inverse_1 = inverse_rms[1]
    inner_1 = (inverse_2 * totals[2:3] - pull * totals[3:4]) / inverse_1
    delta_1 = jnp.where(
        active[1],
        inverse_1 * (grad_in * gain_local)
        - mixed_local[1] * (inverse_1**3 * inner_1 / full_width),
        0.0,
    )

    half = jax.ShapeDtypeStruct((ZL * X, width, full_width // dp_count), BF16)
    kept, given = pl.pallas_call(
        grad_kernel,
        out_shape=(half, half),
        in_specs=[IN_SMEM] + [IN_VMEM] * 3,
        out_specs=(IN_VMEM, IN_VMEM),
        scratch_shapes=[pltpu.VMEM((Y * width, 2 * rows), F32)],
    )(
        lax.axis_index("core").astype(jnp.int32)[None],
        lax.all_gather(states[1], "y", axis=0),
        lax.all_gather(states[2], "y", axis=0),
        jnp.concatenate([delta_1 * factors[1], delta_2 * factors[2]], axis=1).astype(BF16),
    )
    chip_sum = (kept.astype(F32) + shift(given, "core", CORE, 1).astype(F32)).astype(BF16)
    parts = lax.all_to_all(chip_sum, ("zl", "x"), 0, 0)
    return jnp.sum(parts.astype(F32), axis=0)


def solution(mesh):
    fine = Mesh(mesh.devices.reshape(ZL, X, CORE, ZH, Y), ("zl", "x", "core", "zh", "y"))
    return jax.shard_map(
        local,
        mesh=fine,
        in_specs=(
            P(DP, None, MP),
            P(DP, None, MP),
            P(MP, None),
            P(),
            P(DP, None, MP),
            P(),
            P(),
        ),
        out_specs=P(MP, DP),
        check_vma=False,
    )
```

```python
import functools

import jax
import jax.numpy as jnp
from jax import lax
from jax.experimental import pallas as pl
from jax.experimental.layout import Layout, with_layout_constraint
from jax.experimental.pallas import tpu as pltpu
from jax.sharding import Mesh, PartitionSpec as P

MAXR = 3
EPS = 1e-06
ZL, X, CORE, ZH, Y = 3, 4, 2, 4, 8
DP = ("zl", "x", "core")
MP = ("zh", "y")
PIECES = 3
LANES = 128
BF16, F32 = jnp.bfloat16, jnp.float32


def spread(block, axis, count):
    return lax.all_to_all(jnp.broadcast_to(block[None], (count,) + block.shape), axis, 0, 0)


def shift(value, axis, count, by):
    return lax.ppermute(value, axis, [(i, (i + by) % count) for i in range(count)])


def turned(array, axis):
    flipped = lax.rev(array, (axis,))
    double = lax.concatenate([flipped, flipped], axis)
    return lax.dynamic_slice_in_dim(double, ZH - 1 - lax.axis_index("zh"), ZH, axis)


def pack_kernel(weight_ref, pull_ref, out_ref):
    width, padded = weight_ref.shape[0], pull_ref.shape[0]
    third = padded // 3
    lanes = padded - LANES
    out_ref[...] = jnp.zeros_like(out_ref)
    for index in range(ZH * Y):
        first = index * width
        place = index // Y
        out_ref[index % Y, place, :width, :] = weight_ref[:, first : first + LANES]
        for fold in range(3):
            low, high = fold * third, min(fold * third + third, width)
            out_ref[
                index % Y, place, padded : padded + high - low,
                fold * lanes : fold * lanes + width - LANES,
            ] = weight_ref[low:high, first + LANES : first + width]
    for index in range(Y):
        out_ref[index, ZH, :padded, :] = pull_ref[...]


def unpack_kernel(packed_ref, out_ref):
    padded = out_ref.shape[-1]
    third = padded // 3
    lanes = padded - LANES
    for y in range(Y):
        for s in range(ZH):
            out_ref[y, s, :, :LANES] = packed_ref[y, s, :padded, :]
            for fold in range(3):
                out_ref[y, s, fold * third : fold * third + third, LANES:] = packed_ref[
                    y, s, padded : padded + third, fold * lanes : fold * lanes + lanes
                ]


def grad_kernel(core_ref, state_1, state_2, delta_1, delta_2, kept_ref, given_ref):
    core = core_ref[0]
    width, piece = kept_ref.shape[1:]
    first, second = delta_1[...], delta_2[...]

    def outer(delta, state):
        return lax.dot_general(
            delta, state, (((1,), (1,)), ((), ())), preferred_element_type=F32
        )

    def place(out_ref, block, low, value):
        out_ref[block, :, low : low + value.shape[1]] = value

    for part in range(ZH):
        for y in range(Y):
            value = outer(first, state_1[y, part]) + outer(second, state_2[y, part])
            value = value[:width, :width].astype(BF16)
            done = 0
            while done < width:
                column = (part * Y + y) * width + done
                group, low = column // piece, column % piece
                count = min(width - done, piece - low)
                chunk = value[:, done : done + count]
                done += count
                pl.when(core == group % CORE)(
                    functools.partial(place, kept_ref, group // CORE, low, chunk)
                )
                pl.when(core != group % CORE)(
                    functools.partial(place, given_ref, group // CORE, low, chunk)
                )


IN_VMEM = pl.BlockSpec(memory_space=pltpu.VMEM)
IN_SMEM = pl.BlockSpec(memory_space=pltpu.SMEM)


def rotations(block, axis, count):
    return jnp.stack([block] + [shift(block, axis, count, by) for by in range(1, count)])


def to_pieces(sums):
    pieces = []
    for _ in range(PIECES):
        piece = lax.reduce_precision(sums, 8, 7)
        pieces.append(piece.astype(BF16))
        sums = sums - piece
    return jnp.concatenate(pieces)


def from_pieces(rows):
    rows = jnp.sum(rows, axis=tuple(range(rows.ndim - 2)))
    return jnp.sum(rows.reshape(PIECES, -1, rows.shape[-1]), axis=0)


def local(
    prelude_output, init_noise, core_weight, norm_gain, state_cotangent, step_counts, group_table
):
    width, full_width = core_weight.shape
    slot_total, seq_length = init_noise.shape[:2]
    rows = slot_total * seq_length
    dp_count = ZL * X * CORE
    padded = -(-width // 8) * 8
    extra = padded - width
    my_group = lax.axis_index(DP)
    column_first = lax.axis_index(MP) * width
    seq_index = jnp.arange(group_table.shape[0], dtype=jnp.int32)
    real = (jnp.arange(padded) < width)[:, None]

    def columns(array):
        return jnp.pad(array.reshape(rows, width).T, ((0, extra), (0, 0)))

    gain_local = jnp.pad(
        lax.dynamic_slice_in_dim(norm_gain, column_first, width, 0), (0, extra)
    )[:, None]
    scaled = columns(state_cotangent).astype(F32) * gain_local

    packed = pl.pallas_call(
        pack_kernel,
        out_shape=jax.ShapeDtypeStruct((Y, ZH + 1, padded + padded // 3, LANES), BF16),
        in_specs=[IN_VMEM, IN_VMEM],
        out_specs=IN_VMEM,
    )(core_weight, scaled.astype(BF16))
    packed, noise, prelude = lax.optimization_barrier((packed, init_noise, prelude_output))
    packed = lax.all_to_all(packed, "y", 0, 0)
    weight = pl.pallas_call(
        unpack_kernel,
        out_shape=jax.ShapeDtypeStruct((Y, ZH, padded, padded), BF16),
        in_specs=[IN_VMEM],
        out_specs=IN_VMEM,
    )(packed)
    pulled = packed[:, ZH, :padded]
    noise = with_layout_constraint(columns(noise), Layout((0, 1)))
    first_state = turned(rotations(noise, "zh", ZH), 0)
    first_state = with_layout_constraint(first_state, Layout((0, 1, 2)))

    earlier = (group_table[:, None] == group_table[None, :]) & (
        seq_index[None, :] < seq_index[:, None]
    )
    slot_rank = jnp.sum(earlier.astype(jnp.int32), axis=1)
    selected = (group_table[None, :] == my_group) & (
        slot_rank[None, :] == jnp.arange(slot_total, dtype=jnp.int32)[:, None]
    )
    slot_counts = jnp.sum(jnp.where(selected, step_counts[None, :], 0), axis=1)
    token_counts = jnp.repeat(slot_counts, seq_length)
    active = [(turn >= MAXR - token_counts)[None, :] for turn in range(MAXR)]
    gathered = rotations(rotations(prelude, "zl", ZL), "x", X)
    home = seq_index // prelude.shape[0]
    distance = (lax.axis_index("core") - home + CORE) % CORE
    distance = distance * X + (lax.axis_index("x") - home // CORE % X + X) % X
    distance = distance * ZL + (lax.axis_index("zl") - home // (CORE * X) + ZL) % ZL
    arrival = distance * prelude.shape[0] + seq_index % prelude.shape[0]
    chosen = jnp.dot(
        selected.astype(BF16),
        (arrival[:, None] == seq_index[None, :]).astype(BF16),
        preferred_element_type=F32,
    ).astype(BF16)
    own_gains = norm_gain.reshape(ZH, Y, width)
    gains = jnp.pad(
        lax.dynamic_index_in_dim(own_gains, lax.axis_index("y"), 1, False), ((0, 0), (0, extra))
    )
    first_state, weight, gathered, chosen, gains, gain_local, scaled, active = (
        lax.optimization_barrier(
            (first_state, weight, gathered, chosen, gains, gain_local, scaled, active)
        )
    )
    gathered = rotations(gathered, "core", CORE)
    inject = columns(
        jnp.einsum(
            "br,ref->bef",
            chosen,
            gathered.reshape((-1,) + prelude.shape[1:]),
            preferred_element_type=F32,
        )
    )

    def project(state, squares):
        partial = jnp.einsum("yzok,zkt->yot", weight, state, preferred_element_type=F32)
        partial = partial.astype(BF16)
        if squares is None:
            return jnp.sum(lax.all_to_all(partial, "y", 0, 0).astype(F32), axis=0), None
        spare = jnp.broadcast_to(to_pieces(squares)[None], (Y, PIECES, rows))
        partial = jnp.concatenate([partial[:, :width], spare], axis=1)
        parts = lax.all_to_all(partial, "y", 0, 0).astype(F32)
        return jnp.sum(jnp.where(real, parts, 0.0), axis=0), parts[:, width:]

    states, factors, inverse_rms, mixed_local = [first_state], [None], [], []
    squares = None
    for turn in range(MAXR):
        product, spare = project(states[turn], squares)
        if turn:
            inverse = lax.rsqrt(from_pieces(spare) / full_width + EPS)
            inverse_rms.append(inverse)
            factors.append(jnp.where(active[turn - 1], inverse, 1.0))
            product = product * factors[turn]
        mixed = (product + inject).astype(BF16)
        mixed_local.append(mixed.astype(F32))
        if turn + 1 < MAXR:
            whole = spread(mixed, "zh", ZH).astype(F32)
            squares = jnp.sum(whole * whole, axis=(0, 1))[None]
            renewed = (gains[:, :, None] * whole).astype(BF16)
            states.append(jnp.where(active[turn][None], renewed, states[turn]))

    last = mixed_local[2]
    sums = jnp.stack(
        [
            jnp.sum(last * last, axis=0),
            jnp.sum(scaled * last, axis=0),
            jnp.sum(scaled * product, axis=0),
            jnp.sum(last * product, axis=0),
        ]
    )
    sent = jnp.concatenate([mixed, to_pieces(sums)])
    along = spread(sent, "y", Y)

    def transposed(values):
        part = jnp.einsum("yzok,yot->zkt", weight, values, preferred_element_type=F32)
        return part.astype(BF16)

    column_sums = to_pieces(from_pieces(along[:, padded:].astype(F32)))
    column_sums = jnp.broadcast_to(column_sums[None], (ZH,) + column_sums.shape)
    partial = jnp.concatenate([transposed(along[:, :padded]), transposed(pulled), column_sums], 1)
    arrived = lax.all_to_all(partial, "zh", 0, 0).astype(F32)
    through_last = jnp.sum(arrived[:, :padded], axis=0)
    through_scaled = jnp.sum(arrived[:, padded : 2 * padded], axis=0)
    totals = from_pieces(arrived[:, 2 * padded :])

    inverse_2 = lax.rsqrt(totals[0:1] / full_width + EPS)
    pull = inverse_2**3 * totals[1:2] / full_width
    delta_2 = jnp.where(active[2], inverse_2 * scaled - last * pull, 0.0)
    grad_in = inverse_2 * through_scaled - pull * through_last
    inverse_1 = inverse_rms[1]
    inner_1 = (inverse_2 * totals[2:3] - pull * totals[3:4]) / inverse_1
    delta_1 = jnp.where(
        active[1],
        inverse_1 * (grad_in * gain_local)
        - mixed_local[1] * (inverse_1**3 * inner_1 / full_width),
        0.0,
    )

    half = jax.ShapeDtypeStruct((ZL * X, width, full_width // dp_count), BF16)
    kept, given = pl.pallas_call(
        grad_kernel,
        out_shape=(half, half),
        in_specs=[IN_SMEM] + [IN_VMEM] * 4,
        out_specs=(IN_VMEM, IN_VMEM),
    )(
        lax.axis_index("core").astype(jnp.int32)[None],
        lax.all_gather(states[1], "y", axis=0),
        lax.all_gather(states[2], "y", axis=0),
        (delta_1 * factors[1]).astype(BF16),
        (delta_2 * factors[2]).astype(BF16),
    )
    chip_sum = (kept.astype(F32) + shift(given, "core", CORE, 1).astype(F32)).astype(BF16)
    parts = lax.all_to_all(chip_sum, ("zl", "x"), 0, 0)
    return jnp.sum(parts.astype(F32), axis=0)


def solution(mesh):
    fine = Mesh(mesh.devices.reshape(ZL, X, CORE, ZH, Y), ("zl", "x", "core", "zh", "y"))
    return jax.shard_map(
        local,
        mesh=fine,
        in_specs=(
            P(DP, None, MP),
            P(DP, None, MP),
            P(MP, None),
            P(),
            P(DP, None, MP),
            P(),
            P(),
        ),
        out_specs=P(MP, DP),
        check_vma=False,
    )
```

```python
import jax
import jax.numpy as jnp
from jax import lax
from jax.experimental import pallas as pl
from jax.experimental.layout import Layout, with_layout_constraint
from jax.experimental.pallas import tpu as pltpu
from jax.sharding import Mesh, PartitionSpec as P

MAXR = 3
EPS = 1e-06
ZL, X, CORE, ZH, Y = 3, 4, 2, 4, 8
DP = ("zl", "x", "core")
MP = ("zh", "y")
PIECES = 3
LANES = 128
BF16, F32 = jnp.bfloat16, jnp.float32


def spread(block, axis, count):
    return lax.all_to_all(jnp.broadcast_to(block[None], (count,) + block.shape), axis, 0, 0)


def shift(value, axis, count, by):
    return lax.ppermute(value, axis, [(i, (i + by) % count) for i in range(count)])


def turned(array, axis):
    flipped = lax.rev(array, (axis,))
    double = lax.concatenate([flipped, flipped], axis)
    return lax.dynamic_slice_in_dim(double, ZH - 1 - lax.axis_index("zh"), ZH, axis)


def pack_kernel(core_ref, weight_ref, pull_ref, out_ref):
    core = core_ref[0]
    width, padded = weight_ref.shape[0], pull_ref.shape[0]
    half = ZH // CORE
    third = padded // 3
    lanes = padded - LANES
    out_ref[...] = jnp.zeros_like(out_ref)
    for owner in range(CORE):

        @pl.when(core == owner)
        def _():
            for index in range(owner * half * Y, (owner + 1) * half * Y):
                first = index * width
                y, place = index % Y, index // Y % half
                out_ref[y, place, :width, :] = weight_ref[:, first : first + LANES]
                for fold in range(3):
                    low, high = fold * third, min(fold * third + third, width)
                    out_ref[
                        y, place, padded : padded + high - low,
                        fold * lanes : fold * lanes + width - LANES,
                    ] = weight_ref[low:high, first + LANES : first + width]

    for y in range(Y):
        out_ref[y, half, :padded, :] = pull_ref[...]


def unpack_kernel(core_ref, own_ref, other_ref, out_ref):
    core = core_ref[0]
    padded = out_ref.shape[-1]
    half = ZH // CORE
    third = padded // 3
    lanes = padded - LANES
    for owner, ref in ((core, own_ref), (1 - core, other_ref)):
        for s in range(half):
            place = owner * half + s
            for y in range(Y):
                out_ref[y, place, :, :LANES] = ref[y, s, :padded, :]
                for fold in range(3):
                    out_ref[y, place, fold * third : fold * third + third, LANES:] = ref[
                        y, s, padded : padded + third, fold * lanes : fold * lanes + lanes
                    ]


def grad_kernel(core_ref, state_1, state_2, delta_ref, kept_ref, given_ref, flat):
    core = core_ref[0]
    width, piece = kept_ref.shape[1:]
    rows = state_1.shape[-1]
    delta = delta_ref[...]
    for part in range(ZH):
        for step, state in enumerate((state_1, state_2)):
            for y in range(Y):
                flat[y * width : y * width + width, step * rows : step * rows + rows] = state[
                    y, part
                ][:width].astype(F32)
        for block in range(Y * width // piece):
            group = part * (Y * width // piece) + block
            value = lax.dot_general(
                delta,
                flat[block * piece : block * piece + piece, :].astype(BF16),
                (((1,), (1,)), ((), ())),
                preferred_element_type=F32,
            )
            value = value[:width].astype(BF16)

            @pl.when(core == group % CORE)
            def _():
                kept_ref[group // CORE] = value

            @pl.when(core != group % CORE)
            def _():
                given_ref[group // CORE] = value


IN_VMEM = pl.BlockSpec(memory_space=pltpu.VMEM)
IN_SMEM = pl.BlockSpec(memory_space=pltpu.SMEM)


def rotations(block, axis, count):
    return jnp.stack([block] + [shift(block, axis, count, by) for by in range(1, count)])


def to_pieces(sums):
    pieces = []
    for _ in range(PIECES):
        piece = lax.reduce_precision(sums, 8, 7)
        pieces.append(piece.astype(BF16))
        sums = sums - piece
    return jnp.concatenate(pieces)


def from_pieces(rows):
    rows = jnp.sum(rows, axis=tuple(range(rows.ndim - 2)))
    return jnp.sum(rows.reshape(PIECES, -1, rows.shape[-1]), axis=0)


def local(
    prelude_output, init_noise, core_weight, norm_gain, state_cotangent, step_counts, group_table
):
    width, full_width = core_weight.shape
    slot_total, seq_length = init_noise.shape[:2]
    rows = slot_total * seq_length
    dp_count = ZL * X * CORE
    padded = -(-width // 8) * 8
    extra = padded - width
    my_group = lax.axis_index(DP)
    column_first = lax.axis_index(MP) * width
    seq_index = jnp.arange(group_table.shape[0], dtype=jnp.int32)
    real = (jnp.arange(padded) < width)[:, None]

    def columns(array):
        return jnp.pad(array.reshape(rows, width).T, ((0, extra), (0, 0)))

    gain_local = jnp.pad(
        lax.dynamic_slice_in_dim(norm_gain, column_first, width, 0), (0, extra)
    )[:, None]
    scaled = columns(state_cotangent).astype(F32) * gain_local

    core = lax.axis_index("core").astype(jnp.int32)[None]
    packed = pl.pallas_call(
        pack_kernel,
        out_shape=jax.ShapeDtypeStruct((Y, ZH // CORE + 1, padded + padded // 3, LANES), BF16),
        in_specs=[IN_SMEM, IN_VMEM, IN_VMEM],
        out_specs=IN_VMEM,
    )(core, core_weight, scaled.astype(BF16))
    packed, noise, prelude = lax.optimization_barrier((packed, init_noise, prelude_output))
    packed = lax.all_to_all(packed, "y", 0, 0)
    noise = with_layout_constraint(columns(noise), Layout((0, 1)))
    first_state = turned(rotations(noise, "zh", ZH), 0)
    first_state = with_layout_constraint(first_state, Layout((0, 1, 2)))

    gathered = rotations(rotations(prelude, "zl", ZL), "x", X)
    packed, first_state, gathered = lax.optimization_barrier((packed, first_state, gathered))
    weight = pl.pallas_call(
        unpack_kernel,
        out_shape=jax.ShapeDtypeStruct((Y, ZH, padded, padded), BF16),
        in_specs=[IN_SMEM, IN_VMEM, IN_VMEM],
        out_specs=IN_VMEM,
    )(core, packed, shift(packed, "core", CORE, 1))
    pulled = packed[:, ZH // CORE, :padded]

    earlier = (group_table[:, None] == group_table[None, :]) & (
        seq_index[None, :] < seq_index[:, None]
    )
    slot_rank = jnp.sum(earlier.astype(jnp.int32), axis=1)
    selected = (group_table[None, :] == my_group) & (
        slot_rank[None, :] == jnp.arange(slot_total, dtype=jnp.int32)[:, None]
    )
    slot_counts = jnp.sum(jnp.where(selected, step_counts[None, :], 0), axis=1)
    token_counts = jnp.repeat(slot_counts, seq_length)
    active = [(turn >= MAXR - token_counts)[None, :] for turn in range(MAXR)]
    home = seq_index // prelude.shape[0]
    distance = (lax.axis_index("core") - home + CORE) % CORE
    distance = distance * X + (lax.axis_index("x") - home // CORE % X + X) % X
    distance = distance * ZL + (lax.axis_index("zl") - home // (CORE * X) + ZL) % ZL
    arrival = distance * prelude.shape[0] + seq_index % prelude.shape[0]
    chosen = jnp.dot(
        selected.astype(BF16),
        (arrival[:, None] == seq_index[None, :]).astype(BF16),
        preferred_element_type=F32,
    ).astype(BF16)
    own_gains = norm_gain.reshape(ZH, Y, width)
    gains = jnp.pad(
        lax.dynamic_index_in_dim(own_gains, lax.axis_index("y"), 1, False), ((0, 0), (0, extra))
    )
    first_state, weight, gathered, chosen, gains, gain_local, scaled, active = (
        lax.optimization_barrier(
            (first_state, weight, gathered, chosen, gains, gain_local, scaled, active)
        )
    )
    gathered = rotations(gathered, "core", CORE)
    inject = columns(
        jnp.einsum(
            "br,ref->bef",
            chosen,
            gathered.reshape((-1,) + prelude.shape[1:]),
            preferred_element_type=F32,
        )
    )

    def project(state, squares):
        partial = jnp.einsum("yzok,zkt->yot", weight, state, preferred_element_type=F32)
        partial = partial.astype(BF16)
        if squares is None:
            return jnp.sum(lax.all_to_all(partial, "y", 0, 0).astype(F32), axis=0), None
        spare = jnp.broadcast_to(to_pieces(squares)[None], (Y, PIECES, rows))
        partial = jnp.concatenate([partial[:, :width], spare], axis=1)
        parts = lax.all_to_all(partial, "y", 0, 0).astype(F32)
        return jnp.sum(jnp.where(real, parts, 0.0), axis=0), parts[:, width:]

    states, factors, inverse_rms, mixed_local = [first_state], [None], [], []
    squares = None
    for turn in range(MAXR):
        product, spare = project(states[turn], squares)
        if turn:
            inverse = lax.rsqrt(from_pieces(spare) / full_width + EPS)
            inverse_rms.append(inverse)
            factors.append(jnp.where(active[turn - 1], inverse, 1.0))
            product = product * factors[turn]
        mixed = (product + inject).astype(BF16)
        mixed_local.append(mixed.astype(F32))
        if turn + 1 < MAXR:
            whole = spread(mixed, "zh", ZH).astype(F32)
            squares = jnp.sum(whole * whole, axis=(0, 1))[None]
            renewed = (gains[:, :, None] * whole).astype(BF16)
            states.append(jnp.where(active[turn][None], renewed, states[turn]))

    last = mixed_local[2]
    sums = jnp.stack(
        [
            jnp.sum(last * last, axis=0),
            jnp.sum(scaled * last, axis=0),
            jnp.sum(scaled * product, axis=0),
            jnp.sum(last * product, axis=0),
        ]
    )
    sent = jnp.concatenate([mixed, to_pieces(sums)])
    along = spread(sent, "y", Y)

    def transposed(values):
        part = jnp.einsum("yzok,yot->zkt", weight, values, preferred_element_type=F32)
        return part.astype(BF16)

    column_sums = to_pieces(from_pieces(along[:, padded:].astype(F32)))
    column_sums = jnp.broadcast_to(column_sums[None], (ZH,) + column_sums.shape)
    partial = jnp.concatenate([transposed(along[:, :padded]), transposed(pulled), column_sums], 1)
    arrived = lax.all_to_all(partial, "zh", 0, 0).astype(F32)
    through_last = jnp.sum(arrived[:, :padded], axis=0)
    through_scaled = jnp.sum(arrived[:, padded : 2 * padded], axis=0)
    totals = from_pieces(arrived[:, 2 * padded :])

    inverse_2 = lax.rsqrt(totals[0:1] / full_width + EPS)
    pull = inverse_2**3 * totals[1:2] / full_width
    delta_2 = jnp.where(active[2], inverse_2 * scaled - last * pull, 0.0)
    grad_in = inverse_2 * through_scaled - pull * through_last
    inverse_1 = inverse_rms[1]
    inner_1 = (inverse_2 * totals[2:3] - pull * totals[3:4]) / inverse_1
    delta_1 = jnp.where(
        active[1],
        inverse_1 * (grad_in * gain_local)
        - mixed_local[1] * (inverse_1**3 * inner_1 / full_width),
        0.0,
    )

    half = jax.ShapeDtypeStruct((ZL * X, width, full_width // dp_count), BF16)
    kept, given = pl.pallas_call(
        grad_kernel,
        out_shape=(half, half),
        in_specs=[IN_SMEM] + [IN_VMEM] * 3,
        out_specs=(IN_VMEM, IN_VMEM),
        scratch_shapes=[pltpu.VMEM((Y * width, 2 * rows), F32)],
    )(
        core,
        lax.all_gather(states[1], "y", axis=0),
        lax.all_gather(states[2], "y", axis=0),
        jnp.concatenate([delta_1 * factors[1], delta_2 * factors[2]], axis=1).astype(BF16),
    )
    chip_sum = (kept.astype(F32) + shift(given, "core", CORE, 1).astype(F32)).astype(BF16)
    parts = lax.all_to_all(chip_sum, ("zl", "x"), 0, 0)
    return jnp.sum(parts.astype(F32), axis=0)


def solution(mesh):
    fine = Mesh(mesh.devices.reshape(ZL, X, CORE, ZH, Y), ("zl", "x", "core", "zh", "y"))
    return jax.shard_map(
        local,
        mesh=fine,
        in_specs=(
            P(DP, None, MP),
            P(DP, None, MP),
            P(MP, None),
            P(),
            P(DP, None, MP),
            P(),
            P(),
        ),
        out_specs=P(MP, DP),
        check_vma=False,
    )
```

```python
import jax
import jax.numpy as jnp
from jax import lax
from jax.experimental import pallas as pl
from jax.experimental.layout import Layout, with_layout_constraint
from jax.experimental.pallas import tpu as pltpu
from jax.sharding import Mesh, PartitionSpec as P

MAXR = 3
EPS = 1e-06
ZL, X, CORE, ZH, Y = 3, 4, 2, 4, 8
DP = ("zl", "x", "core")
MP = ("zh", "y")
PIECES = 3
LANES = 128
BF16, F32 = jnp.bfloat16, jnp.float32


def spread(block, axis, count):
    return lax.all_to_all(jnp.broadcast_to(block[None], (count,) + block.shape), axis, 0, 0)


def shift(value, axis, count, by):
    return lax.ppermute(value, axis, [(i, (i + by) % count) for i in range(count)])


def turned(array, axis):
    flipped = lax.rev(array, (axis,))
    double = lax.concatenate([flipped, flipped], axis)
    return lax.dynamic_slice_in_dim(double, ZH - 1 - lax.axis_index("zh"), ZH, axis)


def pack_kernel(core_ref, weight_ref, pull_ref, out_ref):
    core = core_ref[0]
    width, padded = weight_ref.shape[0], pull_ref.shape[0]
    half = ZH // CORE
    third = padded // 3
    lanes = padded - LANES
    out_ref[...] = jnp.zeros_like(out_ref)
    for owner in range(CORE):

        @pl.when(core == owner)
        def _():
            for index in range(owner * half * Y, (owner + 1) * half * Y):
                first = index * width
                y, place = index % Y, index // Y % half
                out_ref[y, place, :width, :] = weight_ref[:, first : first + LANES]
                for fold in range(3):
                    low, high = fold * third, min(fold * third + third, width)
                    out_ref[
                        y, place, padded : padded + high - low,
                        fold * lanes : fold * lanes + width - LANES,
                    ] = weight_ref[low:high, first + LANES : first + width]

    for y in range(Y):
        out_ref[y, half, :padded, :] = pull_ref[...]


def unpack_kernel(core_ref, own_ref, other_ref, state_ref, out_ref, product_ref):
    core = core_ref[0]
    padded = out_ref.shape[-1]
    half = ZH // CORE
    third = padded // 3
    lanes = padded - LANES
    for owner, ref in ((core, own_ref), (1 - core, other_ref)):
        for s in range(half):
            place = owner * half + s
            for y in range(Y):
                out_ref[y, place, :, :LANES] = ref[y, s, :padded, :]
                for fold in range(3):
                    out_ref[y, place, fold * third : fold * third + third, LANES:] = ref[
                        y, s, padded : padded + third, fold * lanes : fold * lanes + lanes
                    ]
    for y in range(Y):
        total = jnp.zeros(product_ref.shape[1:], F32)
        for z in range(ZH):
            total = total + jnp.dot(out_ref[y, z], state_ref[z], preferred_element_type=F32)
        product_ref[y] = total.astype(BF16)


def stage_kernel(state_1, state_2, out_ref, flat):
    piece = out_ref.shape[1]
    width = flat.shape[0] // Y
    rows = state_1.shape[-1]
    pieces = flat.shape[0] // piece
    for part in range(ZH):
        for step, state in enumerate((state_1, state_2)):
            for y in range(Y):
                flat[y * width : y * width + width, step * rows : step * rows + rows] = state[
                    y, part
                ][:width].astype(F32)
        for block in range(pieces):
            out_ref[part * pieces + block] = flat[
                block * piece : block * piece + piece, :
            ].astype(BF16)


def grad_kernel(core_ref, delta_ref, blocks_ref, kept_ref, given_ref):
    core = core_ref[0]
    width = kept_ref.shape[1]
    delta = delta_ref[...]
    for pair in range(kept_ref.shape[0]):
        for out_ref, index in ((kept_ref, core), (given_ref, 1 - core)):
            value = lax.dot_general(
                delta,
                blocks_ref[pair * CORE + index],
                (((1,), (1,)), ((), ())),
                preferred_element_type=F32,
            )
            out_ref[pair] = value[:width].astype(BF16)


IN_VMEM = pl.BlockSpec(memory_space=pltpu.VMEM)
IN_SMEM = pl.BlockSpec(memory_space=pltpu.SMEM)


def rotations(block, axis, count):
    return jnp.stack([block] + [shift(block, axis, count, by) for by in range(1, count)])


def to_pieces(sums):
    pieces = []
    for _ in range(PIECES):
        piece = lax.reduce_precision(sums, 8, 7)
        pieces.append(piece.astype(BF16))
        sums = sums - piece
    return jnp.concatenate(pieces)


def from_pieces(rows):
    rows = jnp.sum(rows, axis=tuple(range(rows.ndim - 2)))
    return jnp.sum(rows.reshape(PIECES, -1, rows.shape[-1]), axis=0)


def local(
    prelude_output, init_noise, core_weight, norm_gain, state_cotangent, step_counts, group_table
):
    width, full_width = core_weight.shape
    slot_total, seq_length = init_noise.shape[:2]
    rows = slot_total * seq_length
    dp_count = ZL * X * CORE
    padded = -(-width // 8) * 8
    extra = padded - width
    my_group = lax.axis_index(DP)
    column_first = lax.axis_index(MP) * width
    seq_index = jnp.arange(group_table.shape[0], dtype=jnp.int32)
    real = (jnp.arange(padded) < width)[:, None]

    def columns(array):
        return jnp.pad(array.reshape(rows, width).T, ((0, extra), (0, 0)))

    gain_local = jnp.pad(
        lax.dynamic_slice_in_dim(norm_gain, column_first, width, 0), (0, extra)
    )[:, None]
    scaled = columns(state_cotangent).astype(F32) * gain_local

    core = lax.axis_index("core").astype(jnp.int32)[None]
    packed = pl.pallas_call(
        pack_kernel,
        out_shape=jax.ShapeDtypeStruct((Y, ZH // CORE + 1, padded + padded // 3, LANES), BF16),
        in_specs=[IN_SMEM, IN_VMEM, IN_VMEM],
        out_specs=IN_VMEM,
    )(core, core_weight, scaled.astype(BF16))
    packed, noise, prelude = lax.optimization_barrier((packed, init_noise, prelude_output))
    packed = lax.all_to_all(packed, "y", 0, 0)
    noise = with_layout_constraint(columns(noise), Layout((0, 1)))
    first_state = turned(rotations(noise, "zh", ZH), 0)
    first_state = with_layout_constraint(first_state, Layout((0, 1, 2)))

    gathered = rotations(rotations(prelude, "zl", ZL), "x", X)
    packed, first_state, gathered = lax.optimization_barrier((packed, first_state, gathered))
    weight, first_product = pl.pallas_call(
        unpack_kernel,
        out_shape=(
            jax.ShapeDtypeStruct((Y, ZH, padded, padded), BF16),
            jax.ShapeDtypeStruct((Y, padded, rows), BF16),
        ),
        in_specs=[IN_SMEM] + [IN_VMEM] * 3,
        out_specs=(IN_VMEM, IN_VMEM),
    )(core, packed, shift(packed, "core", CORE, 1), first_state)
    pulled = packed[:, ZH // CORE, :padded]

    earlier = (group_table[:, None] == group_table[None, :]) & (
        seq_index[None, :] < seq_index[:, None]
    )
    slot_rank = jnp.sum(earlier.astype(jnp.int32), axis=1)
    selected = (group_table[None, :] == my_group) & (
        slot_rank[None, :] == jnp.arange(slot_total, dtype=jnp.int32)[:, None]
    )
    slot_counts = jnp.sum(jnp.where(selected, step_counts[None, :], 0), axis=1)
    token_counts = jnp.repeat(slot_counts, seq_length)
    active = [(turn >= MAXR - token_counts)[None, :] for turn in range(MAXR)]
    home = seq_index // prelude.shape[0]
    distance = (lax.axis_index("core") - home + CORE) % CORE
    distance = distance * X + (lax.axis_index("x") - home // CORE % X + X) % X
    distance = distance * ZL + (lax.axis_index("zl") - home // (CORE * X) + ZL) % ZL
    arrival = distance * prelude.shape[0] + seq_index % prelude.shape[0]
    chosen = jnp.dot(
        selected.astype(BF16),
        (arrival[:, None] == seq_index[None, :]).astype(BF16),
        preferred_element_type=F32,
    ).astype(BF16)
    own_gains = norm_gain.reshape(ZH, Y, width)
    gains = jnp.pad(
        lax.dynamic_index_in_dim(own_gains, lax.axis_index("y"), 1, False), ((0, 0), (0, extra))
    )
    first_product, first_state, weight, gathered, chosen, gains, gain_local, scaled, active = (
        lax.optimization_barrier(
            (
                first_product, first_state, weight, gathered, chosen, gains, gain_local, scaled,
                active,
            )
        )
    )
    gathered = rotations(gathered, "core", CORE)
    inject = columns(
        jnp.einsum(
            "br,ref->bef",
            chosen,
            gathered.reshape((-1,) + prelude.shape[1:]),
            preferred_element_type=F32,
        )
    )

    def project(state, squares):
        if squares is None:
            parts = lax.all_to_all(first_product, "y", 0, 0).astype(F32)
            return jnp.sum(parts, axis=0), None
        partial = jnp.einsum("yzok,zkt->yot", weight, state, preferred_element_type=F32)
        partial = partial.astype(BF16)
        spare = jnp.broadcast_to(to_pieces(squares)[None], (Y, PIECES, rows))
        partial = jnp.concatenate([partial[:, :width], spare], axis=1)
        parts = lax.all_to_all(partial, "y", 0, 0).astype(F32)
        return jnp.sum(jnp.where(real, parts, 0.0), axis=0), parts[:, width:]

    states, factors, inverse_rms, mixed_local = [first_state], [None], [], []
    squares = None
    for turn in range(MAXR):
        product, spare = project(states[turn], squares)
        if turn:
            inverse = lax.rsqrt(from_pieces(spare) / full_width + EPS)
            inverse_rms.append(inverse)
            factors.append(jnp.where(active[turn - 1], inverse, 1.0))
            product = product * factors[turn]
        mixed = (product + inject).astype(BF16)
        mixed_local.append(mixed.astype(F32))
        if turn + 1 < MAXR:
            whole = spread(mixed, "zh", ZH).astype(F32)
            squares = jnp.sum(whole * whole, axis=(0, 1))[None]
            renewed = (gains[:, :, None] * whole).astype(BF16)
            states.append(jnp.where(active[turn][None], renewed, states[turn]))

    last = mixed_local[2]
    sums = jnp.stack(
        [
            jnp.sum(last * last, axis=0),
            jnp.sum(scaled * last, axis=0),
            jnp.sum(scaled * product, axis=0),
            jnp.sum(last * product, axis=0),
        ]
    )
    sent = jnp.concatenate([mixed, to_pieces(sums)])
    along = spread(sent, "y", Y)

    def transposed(values):
        part = jnp.einsum("yzok,yot->zkt", weight, values, preferred_element_type=F32)
        return part.astype(BF16)

    column_sums = to_pieces(from_pieces(along[:, padded:].astype(F32)))
    column_sums = jnp.broadcast_to(column_sums[None], (ZH,) + column_sums.shape)
    partial = jnp.concatenate([transposed(along[:, :padded]), transposed(pulled), column_sums], 1)
    piece = full_width // dp_count
    blocks = pl.pallas_call(
        stage_kernel,
        out_shape=jax.ShapeDtypeStruct((dp_count, piece, 2 * rows), BF16),
        in_specs=[IN_VMEM] * 2,
        out_specs=IN_VMEM,
        scratch_shapes=[pltpu.VMEM((Y * width, 2 * rows), F32)],
    )(lax.all_gather(states[1], "y", axis=0), lax.all_gather(states[2], "y", axis=0))
    arrived, blocks = lax.optimization_barrier((lax.all_to_all(partial, "zh", 0, 0), blocks))
    arrived = arrived.astype(F32)
    through_last = jnp.sum(arrived[:, :padded], axis=0)
    through_scaled = jnp.sum(arrived[:, padded : 2 * padded], axis=0)
    totals = from_pieces(arrived[:, 2 * padded :])

    inverse_2 = lax.rsqrt(totals[0:1] / full_width + EPS)
    pull = inverse_2**3 * totals[1:2] / full_width
    delta_2 = jnp.where(active[2], inverse_2 * scaled - last * pull, 0.0)
    grad_in = inverse_2 * through_scaled - pull * through_last
    inverse_1 = inverse_rms[1]
    inner_1 = (inverse_2 * totals[2:3] - pull * totals[3:4]) / inverse_1
    delta_1 = jnp.where(
        active[1],
        inverse_1 * (grad_in * gain_local)
        - mixed_local[1] * (inverse_1**3 * inner_1 / full_width),
        0.0,
    )

    half = jax.ShapeDtypeStruct((ZL * X, width, piece), BF16)
    kept, given = pl.pallas_call(
        grad_kernel,
        out_shape=(half, half),
        in_specs=[IN_SMEM] + [IN_VMEM] * 2,
        out_specs=(IN_VMEM, IN_VMEM),
    )(
        core,
        jnp.concatenate([delta_1 * factors[1], delta_2 * factors[2]], axis=1).astype(BF16),
        blocks,
    )
    chip_sum = (kept.astype(F32) + shift(given, "core", CORE, 1).astype(F32)).astype(BF16)
    parts = lax.all_to_all(chip_sum, ("zl", "x"), 0, 0)
    return jnp.sum(parts.astype(F32), axis=0)


def solution(mesh):
    fine = Mesh(mesh.devices.reshape(ZL, X, CORE, ZH, Y), ("zl", "x", "core", "zh", "y"))
    return jax.shard_map(
        local,
        mesh=fine,
        in_specs=(
            P(DP, None, MP),
            P(DP, None, MP),
            P(MP, None),
            P(),
            P(DP, None, MP),
            P(),
            P(),
        ),
        out_specs=P(MP, DP),
        check_vma=False,
    )
```

```python
import jax
import jax.numpy as jnp
from jax import lax
from jax.experimental import pallas as pl
from jax.experimental.layout import Layout, with_layout_constraint
from jax.experimental.pallas import tpu as pltpu
from jax.sharding import Mesh, PartitionSpec as P

MAXR = 3
EPS = 1e-06
ZL, X, CORE, ZH, Y = 3, 4, 2, 4, 8
DP = ("zl", "x", "core")
MP = ("zh", "y")
PIECES = 3
LANES = 128
BF16, F32 = jnp.bfloat16, jnp.float32


def spread(block, axis, count):
    return lax.all_to_all(jnp.broadcast_to(block[None], (count,) + block.shape), axis, 0, 0)


def shift(value, axis, count, by):
    return lax.ppermute(value, axis, [(i, (i + by) % count) for i in range(count)])


def turned(array, axis):
    flipped = lax.rev(array, (axis,))
    double = lax.concatenate([flipped, flipped], axis)
    return lax.dynamic_slice_in_dim(double, ZH - 1 - lax.axis_index("zh"), ZH, axis)


def pack_kernel(core_ref, weight_ref, pull_ref, out_ref):
    core = core_ref[0]
    width, padded = weight_ref.shape[0], pull_ref.shape[0]
    half = ZH // CORE
    third = padded // 3
    lanes = padded - LANES
    out_ref[...] = jnp.zeros_like(out_ref)
    for owner in range(CORE):

        @pl.when(core == owner)
        def _():
            for index in range(owner * half * Y, (owner + 1) * half * Y):
                first = index * width
                y, place = index % Y, index // Y % half
                out_ref[y, place, :width, :] = weight_ref[:, first : first + LANES]
                for fold in range(3):
                    low, high = fold * third, min(fold * third + third, width)
                    out_ref[
                        y, place, padded : padded + high - low,
                        fold * lanes : fold * lanes + width - LANES,
                    ] = weight_ref[low:high, first + LANES : first + width]

    for y in range(Y):
        out_ref[y, half, :padded, :] = pull_ref[...]


def unpack_kernel(core_ref, own_ref, other_ref, state_ref, out_ref, product_ref):
    core = core_ref[0]
    padded = out_ref.shape[-1]
    half = ZH // CORE
    third = padded // 3
    lanes = padded - LANES
    for owner, ref in ((core, own_ref), (1 - core, other_ref)):
        for s in range(half):
            place = owner * half + s
            for y in range(Y):
                out_ref[y, place, :, :LANES] = ref[y, s, :padded, :]
                for fold in range(3):
                    out_ref[y, place, fold * third : fold * third + third, LANES:] = ref[
                        y, s, padded : padded + third, fold * lanes : fold * lanes + lanes
                    ]
    for y in range(Y):
        total = jnp.zeros(product_ref.shape[1:], F32)
        for z in range(ZH):
            total = total + jnp.dot(out_ref[y, z], state_ref[z], preferred_element_type=F32)
        product_ref[y] = total.astype(BF16)


def stage_kernel(state_1, state_2, out_ref, flat):
    piece = out_ref.shape[1]
    width = flat.shape[0] // Y
    rows = state_1.shape[-1]
    pieces = flat.shape[0] // piece
    for part in range(ZH):
        for step, state in enumerate((state_1, state_2)):
            for y in range(Y):
                flat[y * width : y * width + width, step * rows : step * rows + rows] = state[
                    y, part
                ][:width].astype(F32)
        for block in range(pieces):
            out_ref[part * pieces + block] = flat[
                block * piece : block * piece + piece, :
            ].astype(BF16)


def grad_kernel(core_ref, delta_ref, blocks_ref, kept_ref, given_ref):
    core = core_ref[0]
    width = kept_ref.shape[1]
    delta = delta_ref[...]
    for pair in range(kept_ref.shape[0]):
        for out_ref, index in ((kept_ref, core), (given_ref, 1 - core)):
            value = lax.dot_general(
                delta,
                blocks_ref[pair * CORE + index],
                (((1,), (1,)), ((), ())),
                preferred_element_type=F32,
            )
            out_ref[pair] = value[:width].astype(BF16)


IN_VMEM = pl.BlockSpec(memory_space=pltpu.VMEM)
IN_SMEM = pl.BlockSpec(memory_space=pltpu.SMEM)


def rotations(block, axis, count):
    return jnp.stack([block] + [shift(block, axis, count, by) for by in range(1, count)])


def to_pieces(sums):
    pieces = []
    for _ in range(PIECES):
        piece = lax.reduce_precision(sums, 8, 7)
        pieces.append(piece.astype(BF16))
        sums = sums - piece
    return jnp.concatenate(pieces)


def from_pieces(rows):
    rows = jnp.sum(rows, axis=tuple(range(rows.ndim - 2)))
    return jnp.sum(rows.reshape(PIECES, -1, rows.shape[-1]), axis=0)


def local(
    prelude_output, init_noise, core_weight, norm_gain, state_cotangent, step_counts, group_table
):
    width, full_width = core_weight.shape
    slot_total, seq_length = init_noise.shape[:2]
    rows = slot_total * seq_length
    dp_count = ZL * X * CORE
    padded = -(-width // 8) * 8
    extra = padded - width
    my_group = lax.axis_index(DP)
    column_first = lax.axis_index(MP) * width
    seq_index = jnp.arange(group_table.shape[0], dtype=jnp.int32)
    real = (jnp.arange(padded) < width)[:, None]

    def columns(array):
        return jnp.pad(array.reshape(rows, width).T, ((0, extra), (0, 0)))

    gain_local = jnp.pad(
        lax.dynamic_slice_in_dim(norm_gain, column_first, width, 0), (0, extra)
    )[:, None]
    scaled = columns(state_cotangent).astype(F32) * gain_local

    core = lax.axis_index("core").astype(jnp.int32)[None]
    packed = pl.pallas_call(
        pack_kernel,
        out_shape=jax.ShapeDtypeStruct((Y, ZH // CORE + 1, padded + padded // 3, LANES), BF16),
        in_specs=[IN_SMEM, IN_VMEM, IN_VMEM],
        out_specs=IN_VMEM,
    )(core, core_weight, scaled.astype(BF16))
    packed, noise, prelude = lax.optimization_barrier((packed, init_noise, prelude_output))
    packed = lax.all_to_all(packed, "y", 0, 0)
    noise = with_layout_constraint(columns(noise), Layout((0, 1)))
    first_state = turned(rotations(noise, "zh", ZH), 0)
    first_state = with_layout_constraint(first_state, Layout((0, 1, 2)))

    gathered = rotations(rotations(prelude, "zl", ZL), "x", X)
    packed, first_state, gathered = lax.optimization_barrier((packed, first_state, gathered))
    weight, first_product = pl.pallas_call(
        unpack_kernel,
        out_shape=(
            pltpu.VMEM((Y, ZH, padded, padded), BF16),
            pltpu.VMEM((Y, padded, rows), BF16),
        ),
        in_specs=[IN_SMEM] + [IN_VMEM] * 3,
        out_specs=(IN_VMEM, IN_VMEM),
    )(core, packed, shift(packed, "core", CORE, 1), first_state)
    pulled = packed[:, ZH // CORE, :padded]

    earlier = (group_table[:, None] == group_table[None, :]) & (
        seq_index[None, :] < seq_index[:, None]
    )
    slot_rank = jnp.sum(earlier.astype(jnp.int32), axis=1)
    selected = (group_table[None, :] == my_group) & (
        slot_rank[None, :] == jnp.arange(slot_total, dtype=jnp.int32)[:, None]
    )
    slot_counts = jnp.sum(jnp.where(selected, step_counts[None, :], 0), axis=1)
    token_counts = jnp.repeat(slot_counts, seq_length)
    active = [(turn >= MAXR - token_counts)[None, :] for turn in range(MAXR)]
    home = seq_index // prelude.shape[0]
    distance = (lax.axis_index("core") - home + CORE) % CORE
    distance = distance * X + (lax.axis_index("x") - home // CORE % X + X) % X
    distance = distance * ZL + (lax.axis_index("zl") - home // (CORE * X) + ZL) % ZL
    arrival = distance * prelude.shape[0] + seq_index % prelude.shape[0]
    chosen = jnp.dot(
        selected.astype(BF16),
        (arrival[:, None] == seq_index[None, :]).astype(BF16),
        preferred_element_type=F32,
    ).astype(BF16)
    own_gains = norm_gain.reshape(ZH, Y, width)
    gains = jnp.pad(
        lax.dynamic_index_in_dim(own_gains, lax.axis_index("y"), 1, False), ((0, 0), (0, extra))
    )
    first_product, first_state, weight, gathered, chosen, gains, gain_local, scaled, active = (
        lax.optimization_barrier(
            (
                first_product, first_state, weight, gathered, chosen, gains, gain_local, scaled,
                active,
            )
        )
    )
    gathered = rotations(gathered, "core", CORE)
    inject = columns(
        jnp.einsum(
            "br,ref->bef",
            chosen,
            gathered.reshape((-1,) + prelude.shape[1:]),
            preferred_element_type=F32,
        )
    )

    def project(state, squares):
        if squares is None:
            parts = lax.all_to_all(first_product, "y", 0, 0).astype(F32)
            return jnp.sum(parts, axis=0), None
        partial = jnp.einsum("yzok,zkt->yot", weight, state, preferred_element_type=F32)
        partial = partial.astype(BF16)
        spare = jnp.broadcast_to(to_pieces(squares)[None], (Y, PIECES, rows))
        partial = jnp.concatenate([partial[:, :width], spare], axis=1)
        parts = lax.all_to_all(partial, "y", 0, 0).astype(F32)
        return jnp.sum(jnp.where(real, parts, 0.0), axis=0), parts[:, width:]

    states, factors, inverse_rms, mixed_local = [first_state], [None], [], []
    squares = None
    for turn in range(MAXR):
        product, spare = project(states[turn], squares)
        if turn:
            inverse = lax.rsqrt(from_pieces(spare) / full_width + EPS)
            inverse_rms.append(inverse)
            factors.append(jnp.where(active[turn - 1], inverse, 1.0))
            product = product * factors[turn]
        mixed = (product + inject).astype(BF16)
        mixed_local.append(mixed.astype(F32))
        if turn + 1 < MAXR:
            whole = spread(mixed, "zh", ZH).astype(F32)
            squares = jnp.sum(whole * whole, axis=(0, 1))[None]
            renewed = (gains[:, :, None] * whole).astype(BF16)
            states.append(jnp.where(active[turn][None], renewed, states[turn]))

    last = mixed_local[2]
    sums = jnp.stack(
        [
            jnp.sum(last * last, axis=0),
            jnp.sum(scaled * last, axis=0),
            jnp.sum(scaled * product, axis=0),
            jnp.sum(last * product, axis=0),
        ]
    )
    sent = jnp.concatenate([mixed, to_pieces(sums)])
    along = spread(sent, "y", Y)

    def transposed(values):
        part = jnp.einsum("yzok,yot->zkt", weight, values, preferred_element_type=F32)
        return part.astype(BF16)

    column_sums = to_pieces(from_pieces(along[:, padded:].astype(F32)))
    column_sums = jnp.broadcast_to(column_sums[None], (ZH,) + column_sums.shape)
    partial = jnp.concatenate([transposed(along[:, :padded]), transposed(pulled), column_sums], 1)
    piece = full_width // dp_count
    blocks = pl.pallas_call(
        stage_kernel,
        out_shape=jax.ShapeDtypeStruct((dp_count, piece, 2 * rows), BF16),
        in_specs=[IN_VMEM] * 2,
        out_specs=IN_VMEM,
        scratch_shapes=[pltpu.VMEM((Y * width, 2 * rows), F32)],
    )(lax.all_gather(states[1], "y", axis=0), lax.all_gather(states[2], "y", axis=0))
    arrived, blocks = lax.optimization_barrier((lax.all_to_all(partial, "zh", 0, 0), blocks))
    arrived = arrived.astype(F32)
    through_last = jnp.sum(arrived[:, :padded], axis=0)
    through_scaled = jnp.sum(arrived[:, padded : 2 * padded], axis=0)
    totals = from_pieces(arrived[:, 2 * padded :])

    inverse_2 = lax.rsqrt(totals[0:1] / full_width + EPS)
    pull = inverse_2**3 * totals[1:2] / full_width
    delta_2 = jnp.where(active[2], inverse_2 * scaled - last * pull, 0.0)
    grad_in = inverse_2 * through_scaled - pull * through_last
    inverse_1 = inverse_rms[1]
    inner_1 = (inverse_2 * totals[2:3] - pull * totals[3:4]) / inverse_1
    delta_1 = jnp.where(
        active[1],
        inverse_1 * (grad_in * gain_local)
        - mixed_local[1] * (inverse_1**3 * inner_1 / full_width),
        0.0,
    )

    half = jax.ShapeDtypeStruct((ZL * X, width, piece), BF16)
    kept, given = pl.pallas_call(
        grad_kernel,
        out_shape=(half, half),
        in_specs=[IN_SMEM] + [IN_VMEM] * 2,
        out_specs=(IN_VMEM, IN_VMEM),
    )(
        core,
        jnp.concatenate([delta_1 * factors[1], delta_2 * factors[2]], axis=1).astype(BF16),
        blocks,
    )
    chip_sum = (kept.astype(F32) + shift(given, "core", CORE, 1).astype(F32)).astype(BF16)
    parts = lax.all_to_all(chip_sum, ("zl", "x"), 0, 0)
    return jnp.sum(parts.astype(F32), axis=0)


def solution(mesh):
    fine = Mesh(mesh.devices.reshape(ZL, X, CORE, ZH, Y), ("zl", "x", "core", "zh", "y"))
    return jax.shard_map(
        local,
        mesh=fine,
        in_specs=(
            P(DP, None, MP),
            P(DP, None, MP),
            P(MP, None),
            P(),
            P(DP, None, MP),
            P(),
            P(),
        ),
        out_specs=P(MP, DP),
        check_vma=False,
    )
```
